768 devices in a mesh: row: 24 (over x_lo, z), col: 32 (over y, x_hi, core).
Axes of the slice: x: 4 (x_hi: 2, x_lo: 2; x = x_hi * 2 + x_lo), y: 8, z: 12, core: 2. Of those that a mesh axis runs over, the one named last changes fastest.
Arguments:
- image_emb: bfloat16 [384, 32, 1024], P('row', 'col'), may hold values from -16 to 16
- text_emb: bfloat16 [512, 24, 1024], P('col', 'row'), may hold values from -16 to 16
- logit_scale: float32 [1], replicated, may hold values from 2.5 to 5
Outputs:
- loss: float32 [], replicated
- image_grad: float32 [384, 32, 1024], P('row', 'col')
- text_grad: float32 [512, 24, 1024], P('col', 'row')
The draws below stay inside these ranges and needn't reach their ends.
All inputs are finite; a program needn't handle non-finite values.
Results may differ from the reference program's by a relative error of at most 0.0075.
Values may be sent and summed in bfloat16 or wider, within the bound.
No kernel may reach another device: no remote copies, remote signals or barrier semaphores. Data moves between devices by JAX's collectives and lax.ppermute only.
A program may use at most 32 MiB of HBM per device.

```python
import jax
import jax.numpy as jnp
from jax import lax

E = 1024
BLK = 16
N_ROW = 24
N_COL = 32


def draw_pairs(key):
    total_pairs = BLK * N_ROW * N_COL
    base_key = jax.random.fold_in(key, 7)
    shared = jax.random.truncated_normal(jax.random.fold_in(base_key, 1), -6.0, 6.0, (total_pairs, E), jnp.float32) / jnp.sqrt(1.0 * E)
    noise = jax.random.truncated_normal(jax.random.fold_in(base_key, 2), -6.0, 6.0, (total_pairs, E), jnp.float32) / jnp.sqrt(1.0 * E)
    rising = 1.0 + 2.0 * jnp.arange(total_pairs, dtype=jnp.float32)[:, None] / (total_pairs - 1)
    images = shared * rising
    texts = 0.6 * shared + 0.8 * noise
    return (images, texts)


def draw_image_emb(key, part):
    images, texts = draw_pairs(key)
    return images.reshape(BLK * N_ROW, N_COL, E).astype(jnp.bfloat16)


def draw_text_emb(key, part):
    images, texts = draw_pairs(key)
    return texts.reshape(BLK * N_COL, N_ROW, E).astype(jnp.bfloat16)


def setup_inputs(seed: int = 0) -> dict:
    arg_keys = jax.random.split(jax.random.key(seed), 4)
    image_emb = draw_image_emb(jax.random.fold_in(arg_keys[3], 71), 0)
    text_emb = draw_text_emb(jax.random.fold_in(arg_keys[3], 71), 0)
    logit_scale = jnp.clip(jax.random.uniform(arg_keys[2], (1,), jnp.float32, 2.5, 5.0), 2.5, 5.0)
    return {"image_emb": image_emb, "text_emb": text_emb, "logit_scale": logit_scale}


def reference(image_emb, text_emb, logit_scale):
    total_pairs = BLK * N_ROW * N_COL
    block_rows = BLK * N_COL
    images = image_emb.reshape(total_pairs, E)
    texts = text_emb.reshape(total_pairs, E)
    factor = logit_scale[0]
    image_blocks = images.reshape(N_ROW, block_rows, E)
    col_ids = jnp.arange(total_pairs, dtype=jnp.int32)

    def score_block(index, block):
        scores = factor * jnp.dot(block, texts.T, preferred_element_type=jnp.float32)
        row_ids = index * block_rows + jnp.arange(block_rows, dtype=jnp.int32)
        eye = row_ids[:, None] == col_ids[None, :]
        return scores, eye

    def first_pass(inputs):
        index, block = inputs
        scores, eye = score_block(index, block)
        peak = jnp.max(scores, axis=1)
        row_lse = peak + jnp.log(jnp.sum(jnp.exp(scores - peak[:, None]), axis=1))
        col_peak = jnp.max(scores, axis=0)
        col_sum = jnp.sum(jnp.exp(scores - col_peak[None, :]), axis=0)
        diag = jnp.sum(jnp.where(eye, scores, 0.0))
        return row_lse, col_peak, col_sum, diag

    indices = jnp.arange(N_ROW, dtype=jnp.int32)
    row_lse, col_peaks, col_sums, diags = lax.map(first_pass, (indices, image_blocks))
    overall = jnp.max(col_peaks, axis=0)
    col_lse = overall + jnp.log(jnp.sum(col_sums * jnp.exp(col_peaks - overall[None, :]), axis=0))
    loss = (jnp.sum(row_lse) + jnp.sum(col_lse) - 2.0 * jnp.sum(diags)) / (2.0 * total_pairs)

    def second_pass(carry, inputs):
        index, block, lse_rows = inputs
        scores, eye = score_block(index, block)
        delta = factor * (jnp.exp(scores - lse_rows[:, None]) + jnp.exp(scores - col_lse[None, :]) - 2.0 * eye.astype(jnp.float32))
        delta = delta.astype(jnp.bfloat16)
        grad_rows = jnp.dot(delta, texts, preferred_element_type=jnp.float32)
        carry = carry + jnp.dot(delta.T, block, preferred_element_type=jnp.float32)
        return carry, grad_rows

    start_text = jnp.zeros((total_pairs, E), jnp.float32)
    text_grad, image_rows = lax.scan(second_pass, start_text, (indices, image_blocks, row_lse))
    image_grad = image_rows.reshape(image_emb.shape)
    return loss, image_grad, text_grad.reshape(text_emb.shape)
```

```python
import jax
import jax.numpy as jnp
from jax import lax
from jax.sharding import Mesh, PartitionSpec as P

COL = ("y", "xh", "c")
ROW = ("xl", "z")


def exchange(x, axes):
    return lax.all_to_all(x, axes, 0, 0, tiled=False)


def spread(x, n):
    return jnp.broadcast_to(x[None], (n, *x.shape))


def pieces(v):
    hi = v.astype(jnp.bfloat16)
    rest = v - hi.astype(jnp.float32)
    mid = rest.astype(jnp.bfloat16)
    low = (rest - mid.astype(jnp.float32)).astype(jnp.bfloat16)
    return hi, mid, low


def lse(x, axis):
    peak = jnp.max(x, axis=axis)
    return peak + jnp.log(jnp.sum(jnp.exp(x - jnp.expand_dims(peak, axis)), axis=axis))


def with_scalar(part, v):
    n, b, w = part.shape
    hi, mid, low = pieces(v)
    lane = lax.broadcasted_iota(jnp.int32, (n, b, 128), 2)
    extra = jnp.where(lane == 0, hi, jnp.where(lane == 1, mid, jnp.where(lane == 2, low, jnp.zeros_like(hi))))
    return jnp.concatenate([part, extra], axis=2)


def split_scalar(got):
    w = got.shape[2] - 128
    got = got.astype(jnp.float32)
    total = jnp.sum(got[:, :, :w], axis=0)
    return total, jnp.sum(got[:, 0, w : w + 3])


def shards(image_emb, text_emb, logit_scale):
    n_row = lax.axis_size(ROW)
    n_col = lax.axis_size(COL)
    row_index = lax.axis_index(ROW)
    col_index = lax.axis_index(COL)
    each, _, width = image_emb.shape
    factor = logit_scale[0]
    block_rows, block_cols = each * n_col, each * n_row
    total_pairs = block_rows * n_row
    texts = exchange(spread(text_emb.reshape(each, width), n_row), ROW).reshape(block_cols, width)
    images = exchange(spread(image_emb.reshape(each, width), n_col), COL).reshape(block_rows, width)
    scores = factor * lax.dot_general(images, texts, (((1,), (1,)), ((), ())), preferred_element_type=jnp.float32)
    i = lax.broadcasted_iota(jnp.int32, (block_rows, 1), 0)
    j = lax.broadcasted_iota(jnp.int32, (1, block_cols), 1)
    row_ids = (each * row_index + i % each) * n_col + i // each
    col_ids = (each * col_index + j % each) * n_row + j // each
    eye = row_ids == col_ids
    local_row = lse(scores, 1)
    local_col = lse(scores, 0)
    diag = jnp.sum(jnp.where(eye, scores, 0.0))
    row_pack = jnp.concatenate([local_row, jnp.full((128,), diag)]).reshape(-1, 128)
    col_pack = local_col.reshape(-1, 128)
    row_got = exchange(spread(row_pack, n_col), COL).reshape(n_col, -1)
    col_got = exchange(spread(col_pack, n_row), ROW).reshape(n_row, -1)
    row_lse = lse(row_got[:, :block_rows], 0)
    col_lse = lse(col_got, 0)
    row_loss = jnp.sum(row_lse) - 2.0 * jnp.sum(row_got[:, block_rows])
    col_loss = jnp.sum(col_lse)
    delta = factor * (
        jnp.exp(scores - row_lse[:, None]) + jnp.exp(scores - col_lse[None, :]) - 2.0 * eye.astype(jnp.float32)
    )
    delta = delta.astype(jnp.bfloat16)
    image_part = jnp.dot(delta, texts, preferred_element_type=jnp.float32).astype(jnp.bfloat16)
    text_part = lax.dot_general(delta, images, (((0,), (0,)), ((), ())), preferred_element_type=jnp.float32).astype(jnp.bfloat16)
    text_got = exchange(with_scalar(text_part.reshape(n_row, each, width), row_loss), ROW)
    image_got = exchange(with_scalar(image_part.reshape(n_col, each, width), col_loss), COL)
    text_grad, row_total = split_scalar(text_got)
    image_grad, col_total = split_scalar(image_got)
    loss = (row_total + col_total) / (2.0 * total_pairs)
    return loss, image_grad.reshape(each, 1, width), text_grad.reshape(each, 1, width)


def solution(mesh):
    fine = Mesh(mesh.devices.reshape(2, 12, 8, 2, 2), ROW + COL)
    placed = (P(ROW, COL, None), P(COL, ROW, None), P())
    return jax.shard_map(
        shards,
        mesh=fine,
        in_specs=placed,
        out_specs=(P(), P(ROW, COL, None), P(COL, ROW, None)),
        check_vma=False,
    )
```

```python
import jax
import jax.numpy as jnp
from jax import lax
from jax.sharding import Mesh, PartitionSpec as P


COL = ("y", "xh", "c")
ROW = ("xl", "z")
COL_OUT = ("c", "xh", "y")
ROW_OUT = ("z", "xl")
BF16 = jnp.bfloat16
F32 = jnp.float32


def exchange(x, axes):
    return lax.all_to_all(x, axes, 0, 0, tiled=False)


def spread(x, n):
    return jnp.broadcast_to(x[None], (n, *x.shape))


def shift(x, axis, k):
    n = lax.axis_size(axis)
    return lax.ppermute(x, axis, [(i, (i + k) % n) for i in range(n)])


def pieces(v):
    hi = v.astype(BF16)
    rest = v - hi.astype(F32)
    mid = rest.astype(BF16)
    low = (rest - mid.astype(F32)).astype(BF16)
    return hi, mid, low


def lse(x, axis):
    peak = jnp.max(x, axis=axis)
    return peak + jnp.log(jnp.sum(jnp.exp(x - jnp.expand_dims(peak, axis)), axis=axis))


def with_scalar(part, v):
    n, b, _ = part.shape
    hi, mid, low = pieces(v)
    lane = lax.broadcasted_iota(jnp.int32, (n, b, 128), 2)
    extra = jnp.where(lane == 0, hi, jnp.where(lane == 1, mid, jnp.where(lane == 2, low, jnp.zeros_like(hi))))
    return jnp.concatenate([part, extra], axis=2)


def pick(x, k):
    return lax.dynamic_index_in_dim(x, k, 0, keepdims=False)


def body(image_emb, text_emb, logit_scale):
    n_row, n_col = lax.axis_size(ROW), lax.axis_size(COL)
    n_xl, n_z, n_y, n_xh, n_c = (lax.axis_size(a) for a in ROW + COL)
    row_index, col_index = lax.axis_index(ROW), lax.axis_index(COL)
    y, xh, c = (lax.axis_index(a) for a in COL)
    each, _, width = image_emb.shape
    factor = logit_scale[0]
    block_rows, block_cols = each * n_col, each * n_row
    total_pairs = block_rows * n_row
    images = exchange(spread(image_emb.reshape(each, width), n_col), COL_OUT).reshape(block_rows, width)
    texts = lax.all_gather(text_emb.reshape(each, width), "xl")
    texts = lax.all_gather(texts, "z").reshape(block_cols, width)
    scores = factor * lax.dot_general(images, texts, (((1,), (1,)), ((), ())), preferred_element_type=F32)
    i = lax.broadcasted_iota(jnp.int32, (block_rows, 1), 0)
    j = lax.broadcasted_iota(jnp.int32, (1, block_cols), 1)
    i_dev = (i // each) % n_y * (n_xh * n_c) + (i // (each * n_y)) % n_xh * n_c + i // (each * n_y * n_xh)
    j_dev = (j // each) % n_xl * n_z + j // (each * n_xl)
    row_ids = (each * row_index + i % each) * n_col + i_dev
    col_ids = (each * col_index + j % each) * n_row + j_dev
    eye = row_ids == col_ids
    local_row, local_col = lse(scores, 1), lse(scores, 0)
    diag = jnp.sum(jnp.where(eye, scores, 0.0))
    col_got = exchange(spread(local_col.reshape(-1, 128), n_row), ROW).reshape(n_row, -1)
    col_lse = lse(col_got, 0)
    extra = jnp.concatenate([jnp.full((64,), diag), jnp.full((64,), jnp.sum(col_lse))])
    row_pack = jnp.concatenate([local_row, extra]).reshape(-1, 128)
    row_got = exchange(spread(row_pack, n_col), COL).reshape(n_col, -1)
    row_lse = lse(row_got[:, :block_rows], 0)
    row_loss = jnp.sum(row_lse) - 2.0 * jnp.sum(row_got[:, block_rows])
    col_loss = jnp.sum(row_got[:, block_rows + 64])
    delta = factor * (
        jnp.exp(scores - row_lse[:, None]) + jnp.exp(scores - col_lse[None, :]) - 2.0 * eye.astype(F32)
    )
    delta = delta.astype(BF16)
    text_part = lax.dot_general(delta, images, (((0,), (0,)), ((), ())), preferred_element_type=F32).astype(BF16)
    text_got = exchange(with_scalar(text_part.reshape(n_row, each, width), row_loss), ROW_OUT)
    halves = delta.reshape(n_c, block_rows // n_c, block_cols)
    away = jnp.dot(pick(halves, 1 - c), texts, preferred_element_type=F32).astype(BF16)
    came = shift(away, "c", 1).reshape(n_xh, n_y, each, width)
    here = jnp.dot(pick(halves, c), texts, preferred_element_type=F32).reshape(n_xh, n_y, each, width)
    away = (pick(here, 1 - xh) + pick(came, 1 - xh).astype(F32)).astype(BF16)
    got = shift(away, "xh", 1)
    here = pick(here, xh) + pick(came, xh).astype(F32) + got.astype(F32)
    here = jnp.concatenate([here, here], axis=0)
    ahead = lax.dynamic_slice_in_dim(here, y + 2, 3, 0).astype(BF16)
    behind = lax.dynamic_slice_in_dim(here, y + 5, 2, 0).astype(BF16)
    low = shift(ahead, "y", 3).astype(F32)
    high = shift(behind, "y", 5).astype(F32)
    up = (pick(here, y + 1) + low[2] + high[1]).astype(BF16)
    down = (pick(here, y + n_y - 1) + low[0]).astype(BF16)
    left = shift(up, "y", 1)
    right = shift(down, "y", 7)
    image_grad = pick(here, y) + low[1] + high[0] + left.astype(F32) + right.astype(F32)
    text_got = text_got.astype(F32)
    text_grad = jnp.sum(text_got[:, :, :width], axis=0)
    row_total = jnp.sum(text_got[:, 0, width : width + 3])
    loss = (row_total + col_loss) / (2.0 * total_pairs)
    return loss, image_grad.reshape(each, 1, width), text_grad.reshape(each, 1, width)


def solution(mesh):
    fine = Mesh(mesh.devices.reshape(2, 12, 8, 2, 2), ROW + COL)
    placed = (P(ROW, COL, None), P(COL, ROW, None), P())
    return jax.shard_map(
        body,
        mesh=fine,
        in_specs=placed,
        out_specs=(P(), P(ROW, COL, None), P(COL, ROW, None)),
        check_vma=False,
    )
```

```python
import jax
import jax.numpy as jnp
from jax import lax
from jax.sharding import Mesh, PartitionSpec as P


COL = ("y", "xh", "c")
ROW = ("xl", "z")
COL_OUT = ("c", "xh", "y")
ROW_OUT = ("z", "xl")
BF16 = jnp.bfloat16
F32 = jnp.float32


def exchange(x, axes):
    return lax.all_to_all(x, axes, 0, 0, tiled=False)


def spread(x, n):
    return jnp.broadcast_to(x[None], (n, *x.shape))


def shift(x, axis, k):
    n = lax.axis_size(axis)
    return lax.ppermute(x, axis, [(i, (i + k) % n) for i in range(n)])


def pieces(v):
    hi = v.astype(BF16)
    rest = v - hi.astype(F32)
    mid = rest.astype(BF16)
    low = (rest - mid.astype(F32)).astype(BF16)
    return hi, mid, low


def lse(x, axis):
    peak = jnp.max(x, axis=axis)
    return peak + jnp.log(jnp.sum(jnp.exp(x - jnp.expand_dims(peak, axis)), axis=axis))


def with_scalar(part, v):
    n, b, _ = part.shape
    hi, mid, low = pieces(v)
    lane = lax.broadcasted_iota(jnp.int32, (n, b, 128), 2)
    extra = jnp.where(lane == 0, hi, jnp.where(lane == 1, mid, jnp.where(lane == 2, low, jnp.zeros_like(hi))))
    return jnp.concatenate([part, extra], axis=2)


def pick(x, k):
    return lax.dynamic_index_in_dim(x, k, 0, keepdims=False)


def body(image_emb, text_emb, logit_scale):
    n_row, n_col = lax.axis_size(ROW), lax.axis_size(COL)
    n_xl, n_z, n_y, n_xh, n_c = (lax.axis_size(a) for a in ROW + COL)
    row_index, col_index = lax.axis_index(ROW), lax.axis_index(COL)
    y, xh, c = (lax.axis_index(a) for a in COL)
    each, _, width = image_emb.shape
    factor = logit_scale[0]
    block_rows, block_cols = each * n_col, each * n_row
    total_pairs = block_rows * n_row
    images = exchange(spread(image_emb.reshape(each, width), n_col), COL_OUT).reshape(block_rows, width)
    texts = lax.all_gather(text_emb.reshape(each, width), "xl")
    texts = lax.all_gather(texts, "z").reshape(block_cols, width)
    scores = factor * lax.dot_general(images, texts, (((1,), (1,)), ((), ())), preferred_element_type=F32)
    i = lax.broadcasted_iota(jnp.int32, (block_rows, 1), 0)
    j = lax.broadcasted_iota(jnp.int32, (1, block_cols), 1)
    i_dev = (i // each) % n_y * (n_xh * n_c) + (i // (each * n_y)) % n_xh * n_c + i // (each * n_y * n_xh)
    j_dev = (j // each) % n_xl * n_z + j // (each * n_xl)
    row_ids = (each * row_index + i % each) * n_col + i_dev
    col_ids = (each * col_index + j % each) * n_row + j_dev
    eye = row_ids == col_ids
    local_row, local_col = lse(scores, 1), lse(scores, 0)
    diag = jnp.sum(jnp.where(eye, scores, 0.0))
    col_got = exchange(spread(local_col.reshape(-1, 128), n_row), ROW).reshape(n_row, -1)
    row_pack = jnp.concatenate([local_row, jnp.full((128,), diag)]).reshape(-1, 128)
    row_got = lax.all_gather(row_pack, ("xh", "c")).reshape(n_xh * n_c, -1)
    near_row, near_diag = lse(row_got[:, :block_rows], 0), jnp.sum(row_got[:, block_rows])
    col_lse = lse(col_got, 0)
    extra = jnp.concatenate([jnp.full((64,), near_diag), jnp.full((64,), jnp.sum(col_lse))])
    row_pack = jnp.concatenate([near_row, extra]).reshape(-1, 128)
    row_got = exchange(spread(row_pack, n_y), "y").reshape(n_y, -1)
    row_lse = lse(row_got[:, :block_rows], 0)
    row_loss = jnp.sum(row_lse) - 2.0 * jnp.sum(row_got[:, block_rows])
    col_loss = jnp.full((8, 128), jnp.sum(row_got[:, block_rows + 64]))
    delta = factor * (
        jnp.exp(scores - row_lse[:, None]) + jnp.exp(scores - col_lse[None, :]) - 2.0 * eye.astype(F32)
    )
    delta = delta.astype(BF16)
    halves = delta.reshape(n_c, block_rows // n_c, block_cols)
    away = jnp.dot(pick(halves, 1 - c), texts, preferred_element_type=F32).astype(BF16)
    came = shift(away, "c", 1).reshape(n_xh, n_y, each, width)
    here = jnp.dot(pick(halves, c), texts, preferred_element_type=F32).reshape(n_xh, n_y, each, width)
    away = (pick(here, 1 - xh) + pick(came, 1 - xh).astype(F32)).astype(BF16)
    got = shift(away, "xh", 1)
    text_part = lax.dot_general(delta, images, (((0,), (0,)), ((), ())), preferred_element_type=F32).astype(BF16)
    text_got = exchange(with_scalar(text_part.reshape(n_row, each, width), row_loss), ROW_OUT)
    here = pick(here, xh) + pick(came, xh).astype(F32) + got.astype(F32)
    here = jnp.concatenate([here, here], axis=0)
    ahead = lax.dynamic_slice_in_dim(here, y + 2, 3, 0).astype(BF16)
    behind = lax.dynamic_slice_in_dim(here, y + 5, 2, 0).astype(BF16)
    low = shift(ahead, "y", 3).astype(F32)
    high = shift(behind, "y", 5).astype(F32)
    up = (pick(here, y + 1) + low[2] + high[1]).astype(BF16)
    down = (pick(here, y + n_y - 1) + low[0]).astype(BF16)
    left = shift(up, "y", 1)
    right = shift(down, "y", 7)
    col_loss = col_loss + shift(col_loss, "c", 1)
    col_loss = col_loss + shift(col_loss, "xh", 1)
    image_grad = pick(here, y) + low[1] + high[0] + left.astype(F32) + right.astype(F32)
    text_got = text_got.astype(F32)
    text_grad = jnp.sum(text_got[:, :, :width], axis=0)
    row_total = jnp.sum(text_got[:, 0, width : width + 3])
    loss = (row_total + col_loss[0, 0]) / (2.0 * total_pairs)
    return loss, image_grad.reshape(each, 1, width), text_grad.reshape(each, 1, width)


def solution(mesh):
    fine = Mesh(mesh.devices.reshape(2, 12, 8, 2, 2), ROW + COL)
    placed = (P(ROW, COL, None), P(COL, ROW, None), P())
    return jax.shard_map(
        body,
        mesh=fine,
        in_specs=placed,
        out_specs=(P(), P(ROW, COL, None), P(COL, ROW, None)),
        check_vma=False,
    )
```

```python
import functools

import jax
import jax.numpy as jnp
from jax import lax
from jax.experimental import pallas as pl
from jax.experimental.pallas import tpu as pltpu
from jax.sharding import Mesh, PartitionSpec as P


COL = ("y", "xh", "c")
ROW = ("xl", "z")
N_XL, N_Z, N_Y, N_XH, N_C = 2, 12, 8, 2, 2
N_ROW, N_COL = N_XL * N_Z, N_Y * N_XH * N_C
EACH = 16
WIDTH = 1024
ROWS, COLS = EACH * N_COL, EACH * N_ROW
PAIRS = ROWS * N_ROW
LANES = 128
TAIL = 8
BF16 = jnp.bfloat16
F32 = jnp.float32
VMEM = pl.BlockSpec(memory_space=pltpu.VMEM)
SMEM = pl.BlockSpec(memory_space=pltpu.SMEM)


def exchange(x, axes):
    return lax.all_to_all(x, axes, 0, 0, tiled=False)


def shift(x, axis, k):
    n = lax.axis_size(axis)
    return lax.ppermute(x, axis, [(i, (i + k) % n) for i in range(n)])


def call(kernel, outs, scratch, *args):
    in_specs = [SMEM if a.ndim == 1 else VMEM for a in args]
    return pl.pallas_call(
        kernel,
        out_shape=[jax.ShapeDtypeStruct(s, d) for s, d in outs],
        in_specs=in_specs,
        out_specs=[VMEM] * len(outs),
        scratch_shapes=[pltpu.VMEM(s, d) for s, d in scratch],
        compiler_params=pltpu.CompilerParams(vmem_limit_bytes=24 << 20),
    )(*args)


def lanes(shape):
    return lax.broadcasted_iota(jnp.int32, shape, 1)


def merged(parts):
    peak = functools.reduce(jnp.maximum, parts)
    return peak + jnp.log(sum(jnp.exp(p - peak) for p in parts))


def pieces(v):
    v = jnp.broadcast_to(v, (TAIL, LANES))
    hi = v.astype(BF16).astype(F32)
    mid = (v - hi).astype(BF16).astype(F32)
    low = v - hi - mid
    at = lanes((TAIL, LANES))
    return jnp.where(at == 0, hi, jnp.where(at == 1, mid, jnp.where(at == 2, low, 0.0))).astype(BF16)


def value(tile):
    row = tile.astype(F32)[0:1]
    return jnp.sum(jnp.where(lanes((1, LANES)) < 3, row, 0.0))


def put_tail(ref, at, v):
    ref[at : at + TAIL, :] = jnp.zeros((TAIL, WIDTH), BF16)
    ref[at : at + TAIL, 0:LANES] = pieces(v)


def diagonal(idx, start, count):
    i = lax.broadcasted_iota(jnp.int32, (count, COLS), 0) + start
    j = lax.broadcasted_iota(jnp.int32, (count, COLS), 1)
    i_dev = ((i >> 4) & 7) * (N_XH * N_C) + ((i >> 7) & 1) * N_C + (i >> 8)
    j_dev = ((j >> 4) & 1) * N_Z + (j >> 5)
    row_ids = (EACH * idx[0] + (i & 15)) * N_COL + i_dev
    col_ids = (EACH * idx[1] + (j & 15)) * N_ROW + j_dev
    return row_ids == col_ids


def score_kernel(idx, fac, im, tx, sc, cpack, rpack):
    s = fac[0] * lax.dot_general(im[...], tx[...], (((1,), (1,)), ((), ())), preferred_element_type=F32)
    sc[...] = s
    peak = jnp.max(s, axis=0, keepdims=True)
    col = peak + jnp.log(jnp.sum(jnp.exp(s - peak), axis=0, keepdims=True))
    for k in range(COLS // LANES):
        tile = jnp.broadcast_to(col[:, k * LANES : (k + 1) * LANES], (N_ROW, LANES))
        for n in range(N_ROW):
            cpack[n, k : k + 1, :] = tile[n : n + 1]
    peak = jnp.max(s, axis=1, keepdims=True)
    row = peak + jnp.log(jnp.sum(jnp.exp(s - peak), axis=1, keepdims=True))
    for k in range(ROWS // LANES):
        tile = jnp.broadcast_to(row[k * LANES : (k + 1) * LANES], (LANES, LANES))
        rpack[k : k + 1, :] = tile.T[0:1]
    diag = jnp.sum(jnp.where(diagonal(idx, 0, ROWS), s, 0.0))
    rpack[4:5, :] = jnp.full((1, LANES), diag)


def merge_kernel(col, near, clse, pack):
    lse = merged([col[n] for n in range(N_ROW)])
    total = jnp.zeros((1, LANES), F32)
    for k in range(COLS // LANES):
        clse[:, k * LANES : (k + 1) * LANES] = jnp.broadcast_to(lse[k : k + 1], (8, LANES))
        total = total + lse[k : k + 1]
    total = jnp.full((1, LANES), jnp.sum(total))
    rows = merged([near[n] for n in range(N_XH * N_C)])
    diag = sum(near[n, 4:5, :] for n in range(N_XH * N_C))
    for n in range(N_Y):
        pack[n, 0:4, :] = rows[0:4]
        pack[n, 4:5, :] = diag
        pack[n, 5:6, :] = total


def grad_kernel(idx, fac, sc, im, tx, got, clse, iaway, ihere, taway, there, scal, delta, part):
    rows = merged([got[n] for n in range(N_Y)])[0:4]
    diag = sum(got[n, 4:5, :] for n in range(N_Y))
    total = sum(got[n, 5:6, :] for n in range(N_Y))
    row_loss = jnp.full((1, LANES), jnp.sum(rows)) - 2.0 * diag
    scal[0:8, :] = jnp.broadcast_to(row_loss, (8, LANES))
    scal[8:16, :] = jnp.broadcast_to(total, (8, LANES))
    c, xl = idx[2], idx[5]
    col = clse[0:1, :]
    for k in range(ROWS // LANES):
        s = sc[k * LANES : (k + 1) * LANES, :]
        tile = jnp.broadcast_to(rows[k : k + 1], (LANES, LANES)).T
        lse = jnp.concatenate([tile] * (COLS // LANES), axis=1)
        eye = diagonal(idx, k * LANES, LANES)
        d = jnp.exp(s - lse) + jnp.exp(s - col) - jnp.where(eye, 2.0, 0.0)
        delta[k // 2, (k % 2) * LANES : (k % 2 + 1) * LANES, :] = (fac[0] * d).astype(BF16)
    iaway[0 : ROWS // 2, :] = jnp.dot(delta[1 - c], tx[...], preferred_element_type=F32).astype(BF16)
    put_tail(iaway, ROWS // 2, total)
    whole = delta[...].reshape(ROWS, COLS)
    part[...] = lax.dot_general(
        whole, im[...], (((0,), (0,)), ((), ())), preferred_element_type=F32
    ).reshape(N_Z, N_XL, EACH, WIDTH)
    for z in range(N_Z):
        taway[z * EACH : (z + 1) * EACH, :] = part[z, 1 - xl].astype(BF16)
        there[z * EACH : (z + 1) * EACH, :] = part[z, xl]
    put_tail(taway, COLS // 2, row_loss)
    ihere[...] = jnp.dot(delta[c], tx[...], preferred_element_type=F32)


def across_kernel(idx, scal, here, came, away, keep, out):
    half = ROWS // 4
    xh = idx[3]
    go = pl.multiple_of((1 - xh) * half, half)
    stay = pl.multiple_of(xh * half, half)
    total = scal[8:16, :] + value(came[ROWS // 2 : ROWS // 2 + TAIL, 0:LANES])
    out[...] = total
    away[0:half, :] = (here[pl.ds(go, half), :] + came[pl.ds(go, half), :].astype(F32)).astype(BF16)
    put_tail(away, half, total[0:1])
    keep[...] = here[pl.ds(stay, half), :] + came[pl.ds(stay, half), :].astype(F32)


def text_kernel(scal, here, came, out):
    half = COLS // 2
    loss = scal[0:8, :] + value(came[half : half + TAIL, 0:LANES])
    both = (here[...] + came[0:half, :].astype(F32)).astype(BF16)
    out[:, :, 0:WIDTH] = both.reshape(N_Z, EACH, WIDTH)
    tile = pieces(loss[0:1])
    for z in range(N_Z):
        out[z, 0:8, WIDTH:] = tile
        out[z, 8:16, WIDTH:] = jnp.zeros((8, LANES), BF16)


def ring_kernel(idx, total, keep, got, ahead, behind, near, out):
    y = idx[4]
    half = ROWS // 4
    out[...] = total[...] + value(got[half : half + TAIL, 0:LANES])

    def block(k):
        at = pl.multiple_of(((y + k) & (N_Y - 1)) * EACH, EACH)
        return keep[pl.ds(at, EACH), :] + got[pl.ds(at, EACH), :].astype(F32)

    for n, k in enumerate((2, 3, 4)):
        ahead[n * EACH : (n + 1) * EACH, :] = block(k).astype(BF16)
    for n, k in enumerate((5, 6)):
        behind[n * EACH : (n + 1) * EACH, :] = block(k).astype(BF16)
    for n, k in enumerate((7, 0, 1)):
        near[n * EACH : (n + 1) * EACH, :] = block(k)


def side_kernel(near, low, high, up, down, mid):
    e = EACH
    down[...] = (near[0:e, :] + low[0:e, :].astype(F32)).astype(BF16)
    mid[...] = near[e : 2 * e, :] + low[e : 2 * e, :].astype(F32) + high[0:e, :].astype(F32)
    up[...] = (near[2 * e :, :] + low[2 * e :, :].astype(F32) + high[e:, :].astype(F32)).astype(BF16)


def image_kernel(mid, left, right, out):
    out[...] = (mid[...] + left[...].astype(F32) + right[...].astype(F32)).reshape(EACH, 1, WIDTH)


def final_kernel(got, total, out, loss):
    acc = got[0, :, 0:WIDTH].astype(F32)
    row = got[0, 0:8, WIDTH:].astype(F32)
    for z in range(1, N_Z):
        acc = acc + got[z, :, 0:WIDTH].astype(F32)
        row = row + got[z, 0:8, WIDTH:].astype(F32)
    out[...] = acc.reshape(EACH, 1, WIDTH)
    whole = jnp.sum(jnp.where(lanes((1, LANES)) < 3, row[0:1], 0.0))
    loss[...] = (total[...] + whole) / (2.0 * PAIRS)


def body(image_emb, text_emb, logit_scale):
    places = [lax.axis_index(a) for a in (ROW, COL, "c", "xh", "y", "xl")]
    idx = jnp.stack(places).astype(jnp.int32)
    spread = jnp.broadcast_to(image_emb.reshape(1, EACH, WIDTH), (N_COL, EACH, WIDTH))
    images = exchange(spread, ("c", "xh", "y")).reshape(ROWS, WIDTH)
    texts = lax.all_gather(text_emb.reshape(EACH, WIDTH), "xl")
    texts = lax.all_gather(texts, "z").reshape(COLS, WIDTH)
    scores, cpack, rpack = call(
        score_kernel,
        [((ROWS, COLS), F32), ((N_ROW, 8, LANES), F32), ((8, LANES), F32)],
        [],
        idx, logit_scale, images, texts,
    )
    col_got = exchange(cpack, ROW)
    near = lax.all_gather(rpack, ("xh", "c"))
    col_lse, ypack = call(merge_kernel, [((8, COLS), F32), ((N_Y, 8, LANES), F32)], [], col_got, near)
    row_got = exchange(ypack, "y")
    iaway, ihere, taway, there, scal = call(
        grad_kernel,
        [
            ((ROWS // 2 + TAIL, WIDTH), BF16),
            ((ROWS // 2, WIDTH), F32),
            ((COLS // 2 + TAIL, WIDTH), BF16),
            ((COLS // 2, WIDTH), F32),
            ((16, LANES), F32),
        ],
        [((N_C, ROWS // 2, COLS), BF16), ((N_Z, N_XL, EACH, WIDTH), F32)],
        idx, logit_scale, scores, images, texts, row_got, col_lse,
    )
    tcame = shift(taway, "xl", 1)
    icame = shift(iaway, "c", 1)
    xaway, keep, total = call(
        across_kernel,
        [((ROWS // 4 + TAIL, WIDTH), BF16), ((ROWS // 4, WIDTH), F32), ((8, LANES), F32)],
        [],
        idx, scal, ihere, icame,
    )
    xcame = shift(xaway, "xh", 1)
    (tpack,) = call(text_kernel, [((N_Z, EACH, WIDTH + LANES), BF16)], [], scal, there, tcame)
    text_got = exchange(tpack, "z")
    ahead, behind, near3, total = call(
        ring_kernel,
        [((3 * EACH, WIDTH), BF16), ((2 * EACH, WIDTH), BF16), ((3 * EACH, WIDTH), F32), ((8, LANES), F32)],
        [],
        idx, total, keep, xcame,
    )
    low = shift(ahead, "y", 3)
    high = shift(behind, "y", 5)
    up, down, mid = call(
        side_kernel,
        [((EACH, WIDTH), BF16), ((EACH, WIDTH), BF16), ((EACH, WIDTH), F32)],
        [],
        near3, low, high,
    )
    left = shift(up, "y", 1)
    right = shift(down, "y", 7)
    (image_grad,) = call(image_kernel, [((EACH, 1, WIDTH), F32)], [], mid, left, right)
    text_grad, loss = call(final_kernel, [((EACH, 1, WIDTH), F32), ((8, LANES), F32)], [], text_got, total)
    return loss[0, 0], image_grad, text_grad


def solution(mesh):
    fine = Mesh(mesh.devices.reshape(N_XL, N_Z, N_Y, N_XH, N_C), ROW + COL)
    placed = (P(ROW, COL, None), P(COL, ROW, None), P())
    return jax.shard_map(
        body,
        mesh=fine,
        in_specs=placed,
        out_specs=(P(), P(ROW, COL, None), P(COL, ROW, None)),
        check_vma=False,
    )
```

```python
import functools

import jax
import jax.numpy as jnp
from jax import lax
from jax.experimental import pallas as pl
from jax.experimental.pallas import tpu as pltpu
from jax.sharding import Mesh, PartitionSpec as P


COL = ("y", "xh", "c")
ROW = ("xl", "z")
N_XL, N_Z, N_Y, N_XH, N_C = 2, 12, 8, 2, 2
N_ROW, N_COL = N_XL * N_Z, N_Y * N_XH * N_C
EACH = 16
WIDTH = 1024
ROWS, COLS = EACH * N_COL, EACH * N_ROW
PAIRS = ROWS * N_ROW
LANES = 128
TAIL = 8
BF16 = jnp.bfloat16
F32 = jnp.float32
VMEM = pl.BlockSpec(memory_space=pltpu.VMEM)
SMEM = pl.BlockSpec(memory_space=pltpu.SMEM)


def exchange(x, axes):
    return lax.all_to_all(x, axes, 0, 0, tiled=False)


def shift(x, axis, k):
    n = lax.axis_size(axis)
    return lax.ppermute(x, axis, [(i, (i + k) % n) for i in range(n)])


def call(kernel, outs, scratch, *args):
    in_specs = [SMEM if a.ndim == 1 else VMEM for a in args]
    return pl.pallas_call(
        kernel,
        out_shape=[jax.ShapeDtypeStruct(s, d) for s, d in outs],
        in_specs=in_specs,
        out_specs=[SMEM if s == (1, 1) else VMEM for s, _ in outs],
        scratch_shapes=[pltpu.VMEM(s, d) for s, d in scratch],
        compiler_params=pltpu.CompilerParams(vmem_limit_bytes=24 << 20),
    )(*args)


def lanes(shape):
    return lax.broadcasted_iota(jnp.int32, shape, 1)


def merged(parts):
    peak = functools.reduce(jnp.maximum, parts)
    return peak + jnp.log(sum(jnp.exp(p - peak) for p in parts))


def pieces(v):
    v = jnp.broadcast_to(v, (TAIL, LANES))
    hi = v.astype(BF16).astype(F32)
    mid = (v - hi).astype(BF16).astype(F32)
    low = v - hi - mid
    at = lanes((TAIL, LANES))
    return jnp.where(at == 0, hi, jnp.where(at == 1, mid, jnp.where(at == 2, low, 0.0))).astype(BF16)


def value(tile):
    row = tile.astype(F32)[0:1]
    return jnp.sum(jnp.where(lanes((1, LANES)) < 3, row, 0.0))


def put_tail(ref, at, v):
    ref[at : at + TAIL, :] = jnp.zeros((TAIL, WIDTH), BF16)
    ref[at : at + TAIL, 0:LANES] = pieces(v)


def diagonal(idx, start, count):
    i = lax.broadcasted_iota(jnp.int32, (count, COLS), 0) + start
    j = lax.broadcasted_iota(jnp.int32, (count, COLS), 1)
    i_dev = ((i >> 4) & 7) * (N_XH * N_C) + ((i >> 7) & 1) * N_C + (i >> 8)
    j_dev = ((j >> 4) & 1) * N_Z + (j >> 5)
    row_ids = (EACH * idx[0] + (i & 15)) * N_COL + i_dev
    col_ids = (EACH * idx[1] + (j & 15)) * N_ROW + j_dev
    return row_ids == col_ids


def spread_kernel(block, out):
    tile = block[...]
    for n in range(N_COL):
        out[n] = tile


def score_kernel(idx, fac, im, tx, sc, cpack, rpack):
    s = fac[0] * lax.dot_general(im[...], tx[...], (((1,), (1,)), ((), ())), preferred_element_type=F32)
    sc[...] = s
    peak = jnp.max(s, axis=0, keepdims=True)
    col = peak + jnp.log(jnp.sum(jnp.exp(s - peak), axis=0, keepdims=True))
    for k in range(COLS // LANES):
        tile = jnp.broadcast_to(col[:, k * LANES : (k + 1) * LANES], (N_ROW, LANES))
        for n in range(N_ROW):
            cpack[n, k : k + 1, :] = tile[n : n + 1]
    peak = jnp.max(s, axis=1, keepdims=True)
    row = peak + jnp.log(jnp.sum(jnp.exp(s - peak), axis=1, keepdims=True))
    for k in range(ROWS // LANES):
        tile = jnp.broadcast_to(row[k * LANES : (k + 1) * LANES], (LANES, LANES))
        rpack[k : k + 1, :] = tile.T[0:1]
    diag = jnp.sum(jnp.where(diagonal(idx, 0, ROWS), s, 0.0))
    rpack[4:5, :] = jnp.full((1, LANES), diag)


def merge_kernel(col, near, clse, pack):
    lse = merged([col[n] for n in range(N_ROW)])
    total = jnp.zeros((1, LANES), F32)
    for k in range(COLS // LANES):
        clse[:, k * LANES : (k + 1) * LANES] = jnp.broadcast_to(lse[k : k + 1], (8, LANES))
        total = total + lse[k : k + 1]
    total = jnp.full((1, LANES), jnp.sum(total))
    rows = merged([near[n] for n in range(N_XH * N_C)])
    diag = sum(near[n, 4:5, :] for n in range(N_XH * N_C))
    for n in range(N_Y):
        pack[n, 0:4, :] = rows[0:4]
        pack[n, 4:5, :] = diag
        pack[n, 5:6, :] = total


def grad_kernel(idx, fac, sc, im, tx, got, clse, iaway, ihere, taway, there, scal, delta, part):
    rows = merged([got[n] for n in range(N_Y)])[0:4]
    diag = sum(got[n, 4:5, :] for n in range(N_Y))
    total = sum(got[n, 5:6, :] for n in range(N_Y))
    row_loss = jnp.full((1, LANES), jnp.sum(rows)) - 2.0 * diag
    scal[0:8, :] = jnp.broadcast_to(row_loss, (8, LANES))
    scal[8:16, :] = jnp.broadcast_to(total, (8, LANES))
    c, xl = idx[2], idx[5]
    col = clse[0:1, :]
    for k in range(ROWS // LANES):
        s = sc[k * LANES : (k + 1) * LANES, :]
        tile = jnp.broadcast_to(rows[k : k + 1], (LANES, LANES)).T
        lse = jnp.concatenate([tile] * (COLS // LANES), axis=1)
        eye = diagonal(idx, k * LANES, LANES)
        d = jnp.exp(s - lse) + jnp.exp(s - col) - jnp.where(eye, 2.0, 0.0)
        delta[k // 2, (k % 2) * LANES : (k % 2 + 1) * LANES, :] = (fac[0] * d).astype(BF16)
    iaway[0 : ROWS // 2, :] = jnp.dot(delta[1 - c], tx[...], preferred_element_type=F32).astype(BF16)
    put_tail(iaway, ROWS // 2, total)
    whole = delta[...].reshape(ROWS, COLS)
    part[...] = lax.dot_general(
        whole, im[...], (((0,), (0,)), ((), ())), preferred_element_type=F32
    ).reshape(N_Z, N_XL, EACH, WIDTH)
    for z in range(N_Z):
        taway[z * EACH : (z + 1) * EACH, :] = part[z, 1 - xl].astype(BF16)
        there[z * EACH : (z + 1) * EACH, :] = part[z, xl]
    put_tail(taway, COLS // 2, row_loss)
    ihere[...] = jnp.dot(delta[c], tx[...], preferred_element_type=F32)


def across_kernel(idx, scal, here, came, away, keep, out):
    half = ROWS // 4
    xh = idx[3]
    go = pl.multiple_of((1 - xh) * half, half)
    stay = pl.multiple_of(xh * half, half)
    total = scal[8:16, :] + value(came[ROWS // 2 : ROWS // 2 + TAIL, 0:LANES])
    out[...] = total
    away[0:half, :] = (here[pl.ds(go, half), :] + came[pl.ds(go, half), :].astype(F32)).astype(BF16)
    put_tail(away, half, total[0:1])
    keep[...] = here[pl.ds(stay, half), :] + came[pl.ds(stay, half), :].astype(F32)


def text_kernel(scal, here, came, out):
    half = COLS // 2
    loss = scal[0:8, :] + value(came[half : half + TAIL, 0:LANES])
    both = (here[...] + came[0:half, :].astype(F32)).astype(BF16)
    out[:, :, 0:WIDTH] = both.reshape(N_Z, EACH, WIDTH)
    tile = pieces(loss[0:1])
    for z in range(N_Z):
        out[z, 0:8, WIDTH:] = tile
        out[z, 8:16, WIDTH:] = jnp.zeros((8, LANES), BF16)


def ring_kernel(idx, total, keep, got, ahead, behind, near, out):
    y = idx[4]
    half = ROWS // 4
    out[...] = total[...] + value(got[half : half + TAIL, 0:LANES])

    def block(k):
        at = pl.multiple_of(((y + k) & (N_Y - 1)) * EACH, EACH)
        return keep[pl.ds(at, EACH), :] + got[pl.ds(at, EACH), :].astype(F32)

    for n, k in enumerate((2, 3, 4)):
        ahead[n * EACH : (n + 1) * EACH, :] = block(k).astype(BF16)
    for n, k in enumerate((5, 6)):
        behind[n * EACH : (n + 1) * EACH, :] = block(k).astype(BF16)
    for n, k in enumerate((7, 0, 1)):
        near[n * EACH : (n + 1) * EACH, :] = block(k)


def side_kernel(near, low, high, up, down, mid):
    e = EACH
    down[...] = (near[0:e, :] + low[0:e, :].astype(F32)).astype(BF16)
    mid[...] = near[e : 2 * e, :] + low[e : 2 * e, :].astype(F32) + high[0:e, :].astype(F32)
    up[...] = (near[2 * e :, :] + low[2 * e :, :].astype(F32) + high[e:, :].astype(F32)).astype(BF16)


def image_kernel(mid, left, right, out):
    out[...] = (mid[...] + left[...].astype(F32) + right[...].astype(F32)).reshape(EACH, 1, WIDTH)


def final_kernel(got, total, out, loss):
    acc = got[0, :, 0:WIDTH].astype(F32)
    row = got[0, 0:8, WIDTH:].astype(F32)
    for z in range(1, N_Z):
        acc = acc + got[z, :, 0:WIDTH].astype(F32)
        row = row + got[z, 0:8, WIDTH:].astype(F32)
    out[...] = acc.reshape(EACH, 1, WIDTH)
    whole = jnp.sum(jnp.where(lanes((1, LANES)) < 3, row[0:1], 0.0))
    loss[0, 0] = (jnp.max(total[...]) + whole) / (2.0 * PAIRS)


def body(image_emb, text_emb, logit_scale):
    places = [lax.axis_index(a) for a in (ROW, COL, "c", "xh", "y", "xl")]
    idx = jnp.stack(places).astype(jnp.int32)
    (spread,) = call(spread_kernel, [((N_COL, EACH, WIDTH), BF16)], [], image_emb.reshape(EACH, WIDTH))
    images = exchange(spread, ("c", "xh", "y")).reshape(ROWS, WIDTH)
    texts = lax.all_gather(text_emb.reshape(EACH, WIDTH), "xl")
    texts = lax.all_gather(texts, "z").reshape(COLS, WIDTH)
    scores, cpack, rpack = call(
        score_kernel,
        [((ROWS, COLS), F32), ((N_ROW, 8, LANES), F32), ((8, LANES), F32)],
        [],
        idx, logit_scale, images, texts,
    )
    col_got = exchange(cpack, ROW)
    near = lax.all_gather(rpack, ("xh", "c"))
    col_lse, ypack = call(merge_kernel, [((8, COLS), F32), ((N_Y, 8, LANES), F32)], [], col_got, near)
    row_got = exchange(ypack, "y")
    iaway, ihere, taway, there, scal = call(
        grad_kernel,
        [
            ((ROWS // 2 + TAIL, WIDTH), BF16),
            ((ROWS // 2, WIDTH), F32),
            ((COLS // 2 + TAIL, WIDTH), BF16),
            ((COLS // 2, WIDTH), F32),
            ((16, LANES), F32),
        ],
        [((N_C, ROWS // 2, COLS), BF16), ((N_Z, N_XL, EACH, WIDTH), F32)],
        idx, logit_scale, scores, images, texts, row_got, col_lse,
    )
    tcame = shift(taway, "xl", 1)
    icame = shift(iaway, "c", 1)
    xaway, keep, total = call(
        across_kernel,
        [((ROWS // 4 + TAIL, WIDTH), BF16), ((ROWS // 4, WIDTH), F32), ((8, LANES), F32)],
        [],
        idx, scal, ihere, icame,
    )
    xcame = shift(xaway, "xh", 1)
    (tpack,) = call(text_kernel, [((N_Z, EACH, WIDTH + LANES), BF16)], [], scal, there, tcame)
    text_got = exchange(tpack, "z")
    ahead, behind, near3, total = call(
        ring_kernel,
        [((3 * EACH, WIDTH), BF16), ((2 * EACH, WIDTH), BF16), ((3 * EACH, WIDTH), F32), ((8, LANES), F32)],
        [],
        idx, total, keep, xcame,
    )
    low = shift(ahead, "y", 3)
    high = shift(behind, "y", 5)
    up, down, mid = call(
        side_kernel,
        [((EACH, WIDTH), BF16), ((EACH, WIDTH), BF16), ((EACH, WIDTH), F32)],
        [],
        near3, low, high,
    )
    left = shift(up, "y", 1)
    right = shift(down, "y", 7)
    (image_grad,) = call(image_kernel, [((EACH, 1, WIDTH), F32)], [], mid, left, right)
    text_grad, loss = call(final_kernel, [((EACH, 1, WIDTH), F32), ((1, 1), F32)], [], text_got, total)
    return loss[0, 0], image_grad, text_grad


def solution(mesh):
    fine = Mesh(mesh.devices.reshape(N_XL, N_Z, N_Y, N_XH, N_C), ROW + COL)
    placed = (P(ROW, COL, None), P(COL, ROW, None), P())
    return jax.shard_map(
        body,
        mesh=fine,
        in_specs=placed,
        out_specs=(P(), P(ROW, COL, None), P(COL, ROW, None)),
        check_vma=False,
    )
```

```python
import functools

import jax
import jax.numpy as jnp
from jax import lax
from jax.experimental import pallas as pl
from jax.experimental.pallas import tpu as pltpu
from jax.sharding import Mesh, PartitionSpec as P


COL = ("y", "xh", "c")
ROW = ("xl", "z")
N_XL, N_Z, N_Y, N_XH, N_C = 2, 12, 8, 2, 2
N_ROW, N_COL = N_XL * N_Z, N_Y * N_XH * N_C
EACH = 16
WIDTH = 1024
ROWS, COLS = EACH * N_COL, EACH * N_ROW
PAIRS = ROWS * N_ROW
LANES = 128
TAIL = 8
SLABS = WIDTH // LANES
BF16 = jnp.bfloat16
F32 = jnp.float32
VMEM = pl.BlockSpec(memory_space=pltpu.VMEM)
SMEM = pl.BlockSpec(memory_space=pltpu.SMEM)


def exchange(x, axes):
    return lax.all_to_all(x, axes, 0, 0, tiled=False)


def shift(x, axis, k):
    n = lax.axis_size(axis)
    return lax.ppermute(x, axis, [(i, (i + k) % n) for i in range(n)])


def call(kernel, outs, scratch, *args):
    in_specs = [SMEM if a.ndim == 1 else VMEM for a in args]
    return pl.pallas_call(
        kernel,
        out_shape=[jax.ShapeDtypeStruct(s, d) for s, d in outs],
        in_specs=in_specs,
        out_specs=[SMEM if s == (1, 1) else VMEM for s, _ in outs],
        scratch_shapes=[pltpu.VMEM(s, d) for s, d in scratch],
        compiler_params=pltpu.CompilerParams(vmem_limit_bytes=24 << 20),
    )(*args)


def lanes(shape):
    return lax.broadcasted_iota(jnp.int32, shape, 1)


def merged(parts):
    peak = functools.reduce(jnp.maximum, parts)
    return peak + jnp.log(sum(jnp.exp(p - peak) for p in parts))


def pieces(v):
    v = jnp.broadcast_to(v, (TAIL, LANES))
    hi = v.astype(BF16).astype(F32)
    mid = (v - hi).astype(BF16).astype(F32)
    low = v - hi - mid
    at = lanes((TAIL, LANES))
    return jnp.where(at == 0, hi, jnp.where(at == 1, mid, jnp.where(at == 2, low, 0.0))).astype(BF16)


def value(tile):
    row = tile.astype(F32)[0:1]
    return jnp.sum(jnp.where(lanes((1, LANES)) < 3, row, 0.0))


def put_tail(ref, at, v):
    ref[at : at + TAIL, :] = jnp.zeros((TAIL, WIDTH), BF16)
    ref[at : at + TAIL, 0:LANES] = pieces(v)


def diagonal(idx, start, count):
    i = lax.broadcasted_iota(jnp.int32, (count, COLS), 0) + start
    j = lax.broadcasted_iota(jnp.int32, (count, COLS), 1)
    i_dev = ((i >> 4) & 7) * (N_XH * N_C) + ((i >> 7) & 1) * N_C + (i >> 8)
    j_dev = ((j >> 4) & 1) * N_Z + (j >> 5)
    row_ids = (EACH * idx[0] + (i & 15)) * N_COL + i_dev
    col_ids = (EACH * idx[1] + (j & 15)) * N_ROW + j_dev
    return row_ids == col_ids


def spread_kernel(block, out):
    tile = block[...]
    for n in range(N_COL):
        out[n] = tile


def score_kernel(idx, fac, im, tx, sc, cpack, rpack):
    s = fac[0] * lax.dot_general(im[...], tx[...], (((1,), (1,)), ((), ())), preferred_element_type=F32)
    sc[...] = s
    peak = jnp.max(s, axis=0, keepdims=True)
    col = peak + jnp.log(jnp.sum(jnp.exp(s - peak), axis=0, keepdims=True))
    for k in range(COLS // LANES):
        tile = jnp.broadcast_to(col[:, k * LANES : (k + 1) * LANES], (N_ROW, LANES))
        for n in range(N_ROW):
            cpack[n, k : k + 1, :] = tile[n : n + 1]
    peak = jnp.max(s, axis=1, keepdims=True)
    row = peak + jnp.log(jnp.sum(jnp.exp(s - peak), axis=1, keepdims=True))
    for k in range(ROWS // LANES):
        tile = jnp.broadcast_to(row[k * LANES : (k + 1) * LANES], (LANES, LANES))
        rpack[k : k + 1, :] = tile.T[0:1]
    diag = jnp.sum(jnp.where(diagonal(idx, 0, ROWS), s, 0.0))
    rpack[4:5, :] = jnp.full((1, LANES), diag)


def merge_kernel(col, near, clse, pack):
    lse = merged([col[n] for n in range(N_ROW)])
    total = jnp.zeros((1, LANES), F32)
    for k in range(COLS // LANES):
        clse[:, k * LANES : (k + 1) * LANES] = jnp.broadcast_to(lse[k : k + 1], (8, LANES))
        total = total + lse[k : k + 1]
    total = jnp.full((1, LANES), jnp.sum(total))
    rows = merged([near[n] for n in range(N_XH * N_C)])
    diag = sum(near[n, 4:5, :] for n in range(N_XH * N_C))
    for n in range(N_Y):
        pack[n, 0:4, :] = rows[0:4]
        pack[n, 4:5, :] = diag
        pack[n, 5:6, :] = total


def grad_kernel(idx, fac, sc, im, tx, got, clse, iaway, taway, there, scal, delta, part):
    rows = merged([got[n] for n in range(N_Y)])[0:4]
    diag = sum(got[n, 4:5, :] for n in range(N_Y))
    total = sum(got[n, 5:6, :] for n in range(N_Y))
    row_loss = jnp.full((1, LANES), jnp.sum(rows)) - 2.0 * diag
    scal[0:8, :] = jnp.broadcast_to(row_loss, (8, LANES))
    scal[8:16, :] = jnp.broadcast_to(total, (8, LANES))
    c, xl = idx[2], idx[5]
    col = clse[0:1, :]
    for k in range(ROWS // LANES):
        s = sc[k * LANES : (k + 1) * LANES, :]
        tile = jnp.broadcast_to(rows[k : k + 1], (LANES, LANES)).T
        lse = jnp.concatenate([tile] * (COLS // LANES), axis=1)
        eye = diagonal(idx, k * LANES, LANES)
        d = jnp.exp(s - lse) + jnp.exp(s - col) - jnp.where(eye, 2.0, 0.0)
        delta[k // 2, (k % 2) * LANES : (k % 2 + 1) * LANES, :] = (fac[0] * d).astype(BF16)
    iaway[0 : ROWS // 2, :] = jnp.dot(delta[1 - c], tx[...], preferred_element_type=F32).astype(BF16)
    put_tail(iaway, ROWS // 2, total)
    whole = delta[...].reshape(ROWS, COLS)
    part[...] = lax.dot_general(
        whole, im[...], (((0,), (0,)), ((), ())), preferred_element_type=F32
    ).reshape(N_Z, N_XL, EACH, WIDTH)
    for z in range(N_Z):
        taway[z * EACH : (z + 1) * EACH, :] = part[z, 1 - xl].astype(BF16)
        there[z * EACH : (z + 1) * EACH, :] = part[z, xl]
    put_tail(taway, COLS // 2, row_loss)


def keep_kernel(idx, delta, tx, ihere):
    ihere[...] = jnp.dot(delta[idx[2]], tx[...], preferred_element_type=F32)


def across_kernel(idx, scal, here, came, away, keep, out):
    half = ROWS // 4
    xh = idx[3]
    go = pl.multiple_of((1 - xh) * half, half)
    stay = pl.multiple_of(xh * half, half)
    total = scal[8:16, :] + value(came[ROWS // 2 : ROWS // 2 + TAIL, 0:LANES])
    out[...] = total
    away[0:half, :] = (here[pl.ds(go, half), :] + came[pl.ds(go, half), :].astype(F32)).astype(BF16)
    put_tail(away, half, total[0:1])
    keep[...] = here[pl.ds(stay, half), :] + came[pl.ds(stay, half), :].astype(F32)


def text_kernel(scal, here, came, out):
    half = COLS // 2
    loss = scal[0:8, :] + value(came[half : half + TAIL, 0:LANES])
    both = (here[...] + came[0:half, :].astype(F32)).astype(BF16)
    tile = pieces(loss[0:1])
    for z in range(N_Z):
        for k in range(SLABS):
            out[z, k * EACH : (k + 1) * EACH, :] = both[z * EACH : (z + 1) * EACH, k * LANES : (k + 1) * LANES]
        out[z, SLABS * EACH :, :] = tile


def ring_kernel(idx, total, keep, got, ahead, behind, near, out):
    y = idx[4]
    half = ROWS // 4
    out[...] = total[...] + value(got[half : half + TAIL, 0:LANES])

    def block(k):
        at = pl.multiple_of(((y + k) & (N_Y - 1)) * EACH, EACH)
        return keep[pl.ds(at, EACH), :] + got[pl.ds(at, EACH), :].astype(F32)

    for n, k in enumerate((1, 4, 6)):
        ahead[n * EACH : (n + 1) * EACH, :] = block(k).astype(BF16)
    for n, k in enumerate((7, 2)):
        behind[n * EACH : (n + 1) * EACH, :] = block(k).astype(BF16)
    for n, k in enumerate((0, 3, 5)):
        near[n * EACH : (n + 1) * EACH, :] = block(k)


def side_kernel(near, low, high, up, down, mid):
    e = EACH
    mid[...] = near[0:e, :] + low[0:e, :].astype(F32) + high[0:e, :].astype(F32)
    up[...] = (near[e : 2 * e, :] + low[e : 2 * e, :].astype(F32) + high[e:, :].astype(F32)).astype(BF16)
    down[...] = (near[2 * e :, :] + low[2 * e :, :].astype(F32)).astype(BF16)


def image_kernel(mid, left, right, out):
    out[...] = (mid[...] + left[...].astype(F32) + right[...].astype(F32)).reshape(EACH, 1, WIDTH)


def final_kernel(got, total, out, loss):
    acc = got[0].astype(F32)
    for z in range(1, N_Z):
        acc = acc + got[z].astype(F32)
    row = acc[SLABS * EACH :]
    acc = jnp.concatenate([acc[k * EACH : (k + 1) * EACH] for k in range(SLABS)], axis=1)
    out[...] = acc.reshape(EACH, 1, WIDTH)
    whole = jnp.sum(jnp.where(lanes((1, LANES)) < 3, row[0:1], 0.0))
    loss[0, 0] = (jnp.max(total[...]) + whole) / (2.0 * PAIRS)


def body(image_emb, text_emb, logit_scale):
    places = [lax.axis_index(a) for a in (ROW, COL, "c", "xh", "y", "xl")]
    idx = jnp.stack(places).astype(jnp.int32)
    (spread,) = call(spread_kernel, [((N_COL, EACH, WIDTH), BF16)], [], image_emb.reshape(EACH, WIDTH))
    images = exchange(spread, ("c", "xh", "y")).reshape(ROWS, WIDTH)
    texts = lax.all_gather(text_emb.reshape(EACH, WIDTH), "xl")
    texts = lax.all_gather(texts, "z").reshape(COLS, WIDTH)
    scores, cpack, rpack = call(
        score_kernel,
        [((ROWS, COLS), F32), ((N_ROW, 8, LANES), F32), ((8, LANES), F32)],
        [],
        idx, logit_scale, images, texts,
    )
    col_got = exchange(cpack, ROW)
    near = lax.all_gather(rpack, ("xh", "c"))
    col_lse, ypack = call(merge_kernel, [((8, COLS), F32), ((N_Y, 8, LANES), F32)], [], col_got, near)
    row_got = exchange(ypack, "y")
    iaway, taway, there, scal, delta = call(
        grad_kernel,
        [
            ((ROWS // 2 + TAIL, WIDTH), BF16),
            ((COLS // 2 + TAIL, WIDTH), BF16),
            ((COLS // 2, WIDTH), F32),
            ((16, LANES), F32),
            ((N_C, ROWS // 2, COLS), BF16),
        ],
        [((N_Z, N_XL, EACH, WIDTH), F32)],
        idx, logit_scale, scores, images, texts, row_got, col_lse,
    )
    tcame = shift(taway, "xl", 1)
    icame = shift(iaway, "c", 1)
    (ihere,) = call(keep_kernel, [((ROWS // 2, WIDTH), F32)], [], idx, delta, texts)
    xaway, keep, total = call(
        across_kernel,
        [((ROWS // 4 + TAIL, WIDTH), BF16), ((ROWS // 4, WIDTH), F32), ((8, LANES), F32)],
        [],
        idx, scal, ihere, icame,
    )
    xcame = shift(xaway, "xh", 1)
    (tpack,) = call(text_kernel, [((N_Z, SLABS * EACH + TAIL, LANES), BF16)], [], scal, there, tcame)
    text_got = exchange(tpack, "z")
    ahead, behind, near3, total = call(
        ring_kernel,
        [((3 * EACH, WIDTH), BF16), ((2 * EACH, WIDTH), BF16), ((3 * EACH, WIDTH), F32), ((8, LANES), F32)],
        [],
        idx, total, keep, xcame,
    )
    low = shift(ahead, "y", 1)
    high = shift(behind, "y", 7)
    up, down, mid = call(
        side_kernel,
        [((EACH, WIDTH), BF16), ((EACH, WIDTH), BF16), ((EACH, WIDTH), F32)],
        [],
        near3, low, high,
    )
    left = shift(up, "y", 3)
    right = shift(down, "y", 5)
    (image_grad,) = call(image_kernel, [((EACH, 1, WIDTH), F32)], [], mid, left, right)
    text_grad, loss = call(final_kernel, [((EACH, 1, WIDTH), F32), ((1, 1), F32)], [], text_got, total)
    return loss[0, 0], image_grad, text_grad


def solution(mesh):
    fine = Mesh(mesh.devices.reshape(N_XL, N_Z, N_Y, N_XH, N_C), ROW + COL)
    placed = (P(ROW, COL, None), P(COL, ROW, None), P())
    return jax.shard_map(
        body,
        mesh=fine,
        in_specs=placed,
        out_specs=(P(), P(ROW, COL, None), P(COL, ROW, None)),
        check_vma=False,
    )
```

```python
import functools

import jax
import jax.numpy as jnp
from jax import lax
from jax.experimental import pallas as pl
from jax.experimental.pallas import tpu as pltpu
from jax.sharding import Mesh, PartitionSpec as P


COL = ("y", "xh", "c")
ROW = ("xl", "z")
N_XL, N_Z, N_Y, N_XH, N_C = 2, 12, 8, 2, 2
N_ROW, N_COL = N_XL * N_Z, N_Y * N_XH * N_C
EACH = 16
WIDTH = 1024
ROWS, COLS = EACH * N_COL, EACH * N_ROW
PAIRS = ROWS * N_ROW
LANES = 128
TAIL = 8
SLABS = WIDTH // LANES
BF16 = jnp.bfloat16
F32 = jnp.float32
VMEM = pl.BlockSpec(memory_space=pltpu.VMEM)
SMEM = pl.BlockSpec(memory_space=pltpu.SMEM)


def exchange(x, axes):
    return lax.all_to_all(x, axes, 0, 0, tiled=False)


def shift(x, axis, k):
    n = lax.axis_size(axis)
    return lax.ppermute(x, axis, [(i, (i + k) % n) for i in range(n)])


def call(kernel, outs, scratch, *args):
    in_specs = [SMEM if a.ndim == 1 else VMEM for a in args]
    return pl.pallas_call(
        kernel,
        out_shape=[jax.ShapeDtypeStruct(s, d) for s, d in outs],
        in_specs=in_specs,
        out_specs=[SMEM if s == (1, 1) else VMEM for s, _ in outs],
        scratch_shapes=[pltpu.VMEM(s, d) for s, d in scratch],
        compiler_params=pltpu.CompilerParams(vmem_limit_bytes=24 << 20),
    )(*args)


def lanes(shape):
    return lax.broadcasted_iota(jnp.int32, shape, 1)


def merged(parts):
    peak = functools.reduce(jnp.maximum, parts)
    return peak + jnp.log(sum(jnp.exp(p - peak) for p in parts))


def pieces(v):
    v = jnp.broadcast_to(v, (TAIL, LANES))
    hi = v.astype(BF16).astype(F32)
    mid = (v - hi).astype(BF16).astype(F32)
    low = v - hi - mid
    at = lanes((TAIL, LANES))
    return jnp.where(at == 0, hi, jnp.where(at == 1, mid, jnp.where(at == 2, low, 0.0))).astype(BF16)


def lane_pieces(v, lane):
    v = jnp.broadcast_to(v, (TAIL, LANES))
    hi = v.astype(BF16).astype(F32)
    mid = (v - hi).astype(BF16).astype(F32)
    low = v - hi - mid
    row = lax.broadcasted_iota(jnp.int32, (TAIL, LANES), 0)
    part = jnp.where(row == 0, hi, jnp.where(row == 1, mid, jnp.where(row == 2, low, 0.0)))
    return jnp.where(lanes((TAIL, LANES)) == lane, part, 0.0)


def value(tile):
    row = tile.astype(F32)[0:1]
    return jnp.sum(jnp.where(lanes((1, LANES)) < 3, row, 0.0))


def put_tail(ref, at, v):
    ref[at : at + TAIL, :] = jnp.zeros((TAIL, WIDTH), BF16)
    ref[at : at + TAIL, 0:LANES] = pieces(v)


def diagonal(idx, start, count):
    i = lax.broadcasted_iota(jnp.int32, (count, COLS), 0) + start
    j = lax.broadcasted_iota(jnp.int32, (count, COLS), 1)
    i_dev = ((i >> 4) & 7) * (N_XH * N_C) + ((i >> 7) & 1) * N_C + (i >> 8)
    j_dev = ((j >> 4) & 1) * N_Z + (j >> 5)
    row_ids = (EACH * idx[0] + (i & 15)) * N_COL + i_dev
    col_ids = (EACH * idx[1] + (j & 15)) * N_ROW + j_dev
    return row_ids == col_ids


def spread_kernel(block, out):
    tile = block[...]
    for n in range(N_COL):
        out[n] = tile


def score_kernel(idx, fac, im, tx, sc, cpack, rpack):
    s = fac[0] * lax.dot_general(im[...], tx[...], (((1,), (1,)), ((), ())), preferred_element_type=F32)
    sc[...] = s
    peak = jnp.max(s, axis=0, keepdims=True)
    col = peak + jnp.log(jnp.sum(jnp.exp(s - peak), axis=0, keepdims=True))
    for k in range(COLS // LANES):
        tile = jnp.broadcast_to(col[:, k * LANES : (k + 1) * LANES], (N_Z, LANES))
        for n in range(N_Z):
            cpack[n, k : k + 1, :] = tile[n : n + 1]
    peak = jnp.max(s, axis=1, keepdims=True)
    row = peak + jnp.log(jnp.sum(jnp.exp(s - peak), axis=1, keepdims=True))
    for k in range(ROWS // LANES):
        tile = jnp.broadcast_to(row[k * LANES : (k + 1) * LANES], (LANES, LANES))
        rpack[k : k + 1, :] = tile.T[0:1]
    diag = jnp.sum(jnp.where(diagonal(idx, 0, ROWS), s, 0.0))
    rpack[4:5, :] = jnp.full((1, LANES), diag)


def merge_kernel(col, near, xpack, pack):
    xpack[0:3, :] = merged([col[n] for n in range(N_Z)])[0:3]
    rows = merged([near[n] for n in range(N_XH * N_C)])
    diag = sum(near[n, 4:5, :] for n in range(N_XH * N_C))
    for n in range(N_Y):
        pack[n, 0:4, :] = rows[0:4]
        pack[n, 4:5, :] = diag


def grad_kernel(idx, fac, sc, im, tx, got, gotx, iaway, taway, there, scal, delta, part):
    rows = merged([got[n] for n in range(N_Y)])[0:4]
    diag = sum(got[n, 4:5, :] for n in range(N_Y))
    cols = merged([gotx[n] for n in range(N_XL)])[0:3]
    total = jnp.full((1, LANES), jnp.sum(cols))
    row_loss = jnp.full((1, LANES), jnp.sum(rows)) - 2.0 * diag
    scal[0:8, :] = jnp.broadcast_to(row_loss, (8, LANES))
    scal[8:16, :] = jnp.broadcast_to(total, (8, LANES))
    c, xl = idx[2], idx[5]
    col = jnp.concatenate([cols[k : k + 1] for k in range(COLS // LANES)], axis=1)
    for k in range(ROWS // LANES):
        s = sc[k * LANES : (k + 1) * LANES, :]
        tile = jnp.broadcast_to(rows[k : k + 1], (LANES, LANES)).T
        lse = jnp.concatenate([tile] * (COLS // LANES), axis=1)
        eye = diagonal(idx, k * LANES, LANES)
        d = jnp.exp(s - lse) + jnp.exp(s - col) - jnp.where(eye, 2.0, 0.0)
        delta[k // 2, (k % 2) * LANES : (k % 2 + 1) * LANES, :] = (fac[0] * d).astype(BF16)
    iaway[0 : ROWS // 2, :] = jnp.dot(delta[1 - c], tx[...], preferred_element_type=F32).astype(BF16)
    put_tail(iaway, ROWS // 2, total)
    whole = delta[...].reshape(ROWS, COLS)
    part[...] = lax.dot_general(
        whole, im[...], (((0,), (0,)), ((), ())), preferred_element_type=F32
    ).reshape(N_Z, N_XL, EACH, WIDTH)
    for z in range(N_Z):
        taway[z * EACH : (z + 1) * EACH, :] = part[z, 1 - xl].astype(BF16)
        there[z * EACH : (z + 1) * EACH, :] = part[z, xl]
    put_tail(taway, COLS // 2, row_loss)


def keep_kernel(idx, delta, tx, ihere):
    ihere[...] = jnp.dot(delta[idx[2]], tx[...], preferred_element_type=F32)


def across_kernel(idx, scal, here, came, away, keep, out):
    half = ROWS // 4
    xh = idx[3]
    go = pl.multiple_of((1 - xh) * half, half)
    stay = pl.multiple_of(xh * half, half)
    total = scal[8:16, :] + value(came[ROWS // 2 : ROWS // 2 + TAIL, 0:LANES])
    out[...] = total
    away[0:half, :] = (here[pl.ds(go, half), :] + came[pl.ds(go, half), :].astype(F32)).astype(BF16)
    put_tail(away, half, total[0:1])
    keep[...] = here[pl.ds(stay, half), :] + came[pl.ds(stay, half), :].astype(F32)


def text_kernel(scal, here, came, out):
    half = COLS // 2
    loss = scal[0:8, :] + value(came[half : half + TAIL, 0:LANES])
    both = (here[...] + came[0:half, :].astype(F32)).astype(BF16)
    tile = pieces(loss[0:1])
    for z in range(N_Z):
        for k in range(SLABS):
            out[z, k * EACH : (k + 1) * EACH, :] = both[z * EACH : (z + 1) * EACH, k * LANES : (k + 1) * LANES]
        out[z, SLABS * EACH :, :] = tile


def ring_kernel(idx, total, keep, got, ahead, behind, near, vec):
    y = idx[4]
    half = ROWS // 4
    whole = total[0:1, :] + value(got[half : half + TAIL, 0:LANES])
    tile = lane_pieces(whole, y)
    vec[...] = tile
    for ref, at in ((ahead, 3 * EACH), (behind, 2 * EACH)):
        ref[at:, :] = jnp.zeros((TAIL, WIDTH), BF16)
        ref[at:, 0:LANES] = tile.astype(BF16)

    def block(k):
        at = pl.multiple_of(((y + k) & (N_Y - 1)) * EACH, EACH)
        return keep[pl.ds(at, EACH), :] + got[pl.ds(at, EACH), :].astype(F32)

    for n, k in enumerate((1, 4, 6)):
        ahead[n * EACH : (n + 1) * EACH, :] = block(k).astype(BF16)
    for n, k in enumerate((7, 2)):
        behind[n * EACH : (n + 1) * EACH, :] = block(k).astype(BF16)
    for n, k in enumerate((0, 3, 5)):
        near[n * EACH : (n + 1) * EACH, :] = block(k)


def side_kernel(near, vec, low, high, up, down, mid, out):
    e = EACH
    mid[...] = near[0:e, :] + low[0:e, :].astype(F32) + high[0:e, :].astype(F32)
    up[0:e, :] = (near[e : 2 * e, :] + low[e : 2 * e, :].astype(F32) + high[e : 2 * e, :].astype(F32)).astype(BF16)
    down[0:e, :] = (near[2 * e :, :] + low[2 * e : 3 * e, :].astype(F32)).astype(BF16)
    tile = vec[...] + low[3 * e :, 0:LANES].astype(F32) + high[2 * e :, 0:LANES].astype(F32)
    out[...] = tile
    for ref in (up, down):
        ref[e:, :] = jnp.zeros((TAIL, WIDTH), BF16)
        ref[e:, 0:LANES] = tile.astype(BF16)


def final_kernel(idx, mid, vec, left, right, got, image, text, loss):
    e = EACH
    image[...] = (mid[...] + left[0:e, :].astype(F32) + right[0:e, :].astype(F32)).reshape(e, 1, WIDTH)
    far = (idx[4] + N_Y // 2) & (N_Y - 1)
    new = jnp.where(lanes((TAIL, LANES)) == far, 0.0, left[e:, 0:LANES].astype(F32))
    tile = vec[...] + new + right[e:, 0:LANES].astype(F32)
    col_total = jnp.sum(tile[0:1] + tile[1:2] + tile[2:3])
    acc = got[0].astype(F32)
    for z in range(1, N_Z):
        acc = acc + got[z].astype(F32)
    row = acc[SLABS * e :]
    acc = jnp.concatenate([acc[k * e : (k + 1) * e] for k in range(SLABS)], axis=1)
    text[...] = acc.reshape(e, 1, WIDTH)
    row_total = jnp.sum(jnp.where(lanes((1, LANES)) < 3, row[0:1], 0.0))
    loss[0, 0] = (col_total + row_total) / (2.0 * PAIRS)


def body(image_emb, text_emb, logit_scale):
    places = [lax.axis_index(a) for a in (ROW, COL, "c", "xh", "y", "xl")]
    idx = jnp.stack(places).astype(jnp.int32)
    (spread,) = call(spread_kernel, [((N_COL, EACH, WIDTH), BF16)], [], image_emb.reshape(EACH, WIDTH))
    images = exchange(spread, ("c", "xh", "y")).reshape(ROWS, WIDTH)
    texts = lax.all_gather(text_emb.reshape(EACH, WIDTH), "xl")
    texts = lax.all_gather(texts, "z").reshape(COLS, WIDTH)
    scores, cpack, rpack = call(
        score_kernel,
        [((ROWS, COLS), F32), ((N_Z, 8, LANES), F32), ((8, LANES), F32)],
        [],
        idx, logit_scale, images, texts,
    )
    col_got = exchange(cpack, "z")
    near = lax.all_gather(rpack, ("xh", "c"))
    xpack, ypack = call(merge_kernel, [((8, LANES), F32), ((N_Y, 8, LANES), F32)], [], col_got, near)
    row_got = exchange(ypack, "y")
    col_got = lax.all_gather(xpack, "xl")
    iaway, taway, there, scal, delta = call(
        grad_kernel,
        [
            ((ROWS // 2 + TAIL, WIDTH), BF16),
            ((COLS // 2 + TAIL, WIDTH), BF16),
            ((COLS // 2, WIDTH), F32),
            ((16, LANES), F32),
            ((N_C, ROWS // 2, COLS), BF16),
        ],
        [((N_Z, N_XL, EACH, WIDTH), F32)],
        idx, logit_scale, scores, images, texts, row_got, col_got,
    )
    tcame = shift(taway, "xl", 1)
    icame = shift(iaway, "c", 1)
    (ihere,) = call(keep_kernel, [((ROWS // 2, WIDTH), F32)], [], idx, delta, texts)
    xaway, keep, total = call(
        across_kernel,
        [((ROWS // 4 + TAIL, WIDTH), BF16), ((ROWS // 4, WIDTH), F32), ((8, LANES), F32)],
        [],
        idx, scal, ihere, icame,
    )
    xcame = shift(xaway, "xh", 1)
    (tpack,) = call(text_kernel, [((N_Z, SLABS * EACH + TAIL, LANES), BF16)], [], scal, there, tcame)
    text_got = exchange(tpack, "z")
    ahead, behind, near3, vec = call(
        ring_kernel,
        [
            ((3 * EACH + TAIL, WIDTH), BF16),
            ((2 * EACH + TAIL, WIDTH), BF16),
            ((3 * EACH, WIDTH), F32),
            ((TAIL, LANES), F32),
        ],
        [],
        idx, total, keep, xcame,
    )
    low = shift(ahead, "y", 1)
    high = shift(behind, "y", 7)
    up, down, mid, vec = call(
        side_kernel,
        [((EACH + TAIL, WIDTH), BF16), ((EACH + TAIL, WIDTH), BF16), ((EACH, WIDTH), F32), ((TAIL, LANES), F32)],
        [],
        near3, vec, low, high,
    )
    left = shift(up, "y", 3)
    right = shift(down, "y", 5)
    image_grad, text_grad, loss = call(
        final_kernel,
        [((EACH, 1, WIDTH), F32), ((EACH, 1, WIDTH), F32), ((1, 1), F32)],
        [],
        idx, mid, vec, left, right, text_got,
    )
    return loss[0, 0], image_grad, text_grad


def solution(mesh):
    fine = Mesh(mesh.devices.reshape(N_XL, N_Z, N_Y, N_XH, N_C), ROW + COL)
    placed = (P(ROW, COL, None), P(COL, ROW, None), P())
    return jax.shard_map(
        body,
        mesh=fine,
        in_specs=placed,
        out_specs=(P(), P(ROW, COL, None), P(COL, ROW, None)),
        check_vma=False,
    )
```

```python
import functools

import jax
import jax.numpy as jnp
from jax import lax
from jax.experimental import pallas as pl
from jax.experimental.pallas import tpu as pltpu
from jax.sharding import Mesh, PartitionSpec as P


COL = ("y", "xh", "c")
ROW = ("xl", "z")
N_XL, N_Z, N_Y, N_XH, N_C = 2, 12, 8, 2, 2
N_ROW, N_COL = N_XL * N_Z, N_Y * N_XH * N_C
EACH = 16
WIDTH = 1024
ROWS, COLS = EACH * N_COL, EACH * N_ROW
PAIRS = ROWS * N_ROW
LANES = 128
TAIL = 8
SLABS = WIDTH // LANES
BF16 = jnp.bfloat16
F32 = jnp.float32
VMEM = pl.BlockSpec(memory_space=pltpu.VMEM)
SMEM = pl.BlockSpec(memory_space=pltpu.SMEM)


def exchange(x, axes):
    return lax.all_to_all(x, axes, 0, 0, tiled=False)


def shift(x, axis, k):
    n = lax.axis_size(axis)
    return lax.ppermute(x, axis, [(i, (i + k) % n) for i in range(n)])


def call(kernel, outs, scratch, *args):
    in_specs = [SMEM if a.ndim == 1 else VMEM for a in args]
    return pl.pallas_call(
        kernel,
        out_shape=[jax.ShapeDtypeStruct(s, d) for s, d in outs],
        in_specs=in_specs,
        out_specs=[SMEM if s == (1, 1) else VMEM for s, _ in outs],
        scratch_shapes=[pltpu.VMEM(s, d) for s, d in scratch],
        compiler_params=pltpu.CompilerParams(vmem_limit_bytes=24 << 20),
    )(*args)


def lanes(shape):
    return lax.broadcasted_iota(jnp.int32, shape, 1)


def merged(parts):
    peak = functools.reduce(jnp.maximum, parts)
    return peak + jnp.log(sum(jnp.exp(p - peak) for p in parts))


def pieces(v):
    v = jnp.broadcast_to(v, (TAIL, LANES))
    hi = v.astype(BF16).astype(F32)
    mid = (v - hi).astype(BF16).astype(F32)
    low = v - hi - mid
    at = lanes((TAIL, LANES))
    return jnp.where(at == 0, hi, jnp.where(at == 1, mid, jnp.where(at == 2, low, 0.0))).astype(BF16)


def value(tile):
    row = tile.astype(F32)[0:1]
    return jnp.sum(jnp.where(lanes((1, LANES)) < 3, row, 0.0))


def put_tail(ref, at, v):
    ref[at : at + TAIL, :] = jnp.zeros((TAIL, WIDTH), BF16)
    ref[at : at + TAIL, 0:LANES] = pieces(v)


def diagonal(idx, start, count):
    z, c, y, xh, xl = (idx[n] for n in range(5))
    i = lax.broadcasted_iota(jnp.int32, (count, COLS), 0) + start
    j = lax.broadcasted_iota(jnp.int32, (count, COLS), 1)
    i_dev = ((i >> 4) & 7) * (N_XH * N_C) + ((i >> 7) & 1) * N_C + c
    i_row = (i >> 8) * N_Z + z
    j_dev = xl * N_Z + (j >> 5)
    j_col = y * (N_XH * N_C) + xh * N_C + ((j >> 4) & 1)
    row_ids = (EACH * i_row + (i & 15)) * N_COL + i_dev
    col_ids = (EACH * j_col + (j & 15)) * N_ROW + j_dev
    return row_ids == col_ids


def spread_kernel(block, out):
    tile = block[...]
    for n in range(N_COL):
        out[n] = tile


def score_kernel(idx, fac, im, tx, sc, cpack, rpack):
    s = fac[0] * lax.dot_general(im[...], tx[...], (((1,), (1,)), ((), ())), preferred_element_type=F32)
    sc[...] = s
    peak = jnp.max(s, axis=0, keepdims=True)
    col = peak + jnp.log(jnp.sum(jnp.exp(s - peak), axis=0, keepdims=True))
    for k in range(COLS // LANES):
        tile = jnp.broadcast_to(col[:, k * LANES : (k + 1) * LANES], (N_ROW, LANES))
        for n in range(N_ROW):
            cpack[n, k : k + 1, :] = tile[n : n + 1]
    peak = jnp.max(s, axis=1, keepdims=True)
    row = peak + jnp.log(jnp.sum(jnp.exp(s - peak), axis=1, keepdims=True))
    for k in range(ROWS // LANES):
        tile = jnp.broadcast_to(row[k * LANES : (k + 1) * LANES], (LANES, LANES))
        rpack[k : k + 1, :] = tile.T[0:1]
    diag = jnp.sum(jnp.where(diagonal(idx, 0, ROWS), s, 0.0))
    rpack[4:5, :] = jnp.full((1, LANES), diag)


def merge_kernel(col, near, clse, pack):
    lse = merged([col[n] for n in range(N_ROW)])
    total = jnp.zeros((1, LANES), F32)
    for k in range(COLS // LANES):
        clse[:, k * LANES : (k + 1) * LANES] = jnp.broadcast_to(lse[k : k + 1], (8, LANES))
        total = total + lse[k : k + 1]
    total = jnp.full((1, LANES), jnp.sum(total))
    rows = merged([near[n] for n in range(N_XL * N_XH)])
    diag = sum(near[n, 4:5, :] for n in range(N_XL * N_XH))
    for n in range(N_Y):
        pack[n, 0:4, :] = rows[0:4]
        pack[n, 4:5, :] = diag
        pack[n, 5:6, :] = total


def grad_kernel(idx, fac, sc, im, tx, got, clse, iaway, taway, there, scal, delta, part):
    rows = merged([got[n] for n in range(N_Y)])[0:4]
    diag = sum(got[n, 4:5, :] for n in range(N_Y))
    total = sum(got[n, 5:6, :] for n in range(N_Y))
    row_loss = jnp.full((1, LANES), jnp.sum(rows)) - 2.0 * diag
    scal[0:8, :] = jnp.broadcast_to(row_loss, (8, LANES))
    scal[8:16, :] = jnp.broadcast_to(total, (8, LANES))
    c, xl = idx[1], idx[4]
    col = clse[0:1, :]
    for k in range(ROWS // LANES):
        s = sc[k * LANES : (k + 1) * LANES, :]
        tile = jnp.broadcast_to(rows[k : k + 1], (LANES, LANES)).T
        lse = jnp.concatenate([tile] * (COLS // LANES), axis=1)
        eye = diagonal(idx, k * LANES, LANES)
        d = jnp.exp(s - lse) + jnp.exp(s - col) - jnp.where(eye, 2.0, 0.0)
        delta[k // 2, (k % 2) * LANES : (k % 2 + 1) * LANES, :] = (fac[0] * d).astype(BF16)
    iaway[0 : ROWS // 2, :] = jnp.dot(delta[1 - xl], tx[...], preferred_element_type=F32).astype(BF16)
    put_tail(iaway, ROWS // 2, total)
    whole = delta[...].reshape(ROWS, COLS)
    part[...] = lax.dot_general(
        whole, im[...], (((0,), (0,)), ((), ())), preferred_element_type=F32
    ).reshape(N_Z, N_C, EACH, WIDTH)
    for z in range(N_Z):
        taway[z * EACH : (z + 1) * EACH, :] = part[z, 1 - c].astype(BF16)
        there[z * EACH : (z + 1) * EACH, :] = part[z, c]
    put_tail(taway, COLS // 2, row_loss)


def keep_kernel(idx, delta, tx, ihere):
    ihere[...] = jnp.dot(delta[idx[4]], tx[...], preferred_element_type=F32)


def across_kernel(idx, scal, here, came, away, keep, out):
    half = ROWS // 4
    xh = idx[3]
    go = pl.multiple_of((1 - xh) * half, half)
    stay = pl.multiple_of(xh * half, half)
    total = scal[8:16, :] + value(came[ROWS // 2 : ROWS // 2 + TAIL, 0:LANES])
    out[...] = total
    away[0:half, :] = (here[pl.ds(go, half), :] + came[pl.ds(go, half), :].astype(F32)).astype(BF16)
    put_tail(away, half, total[0:1])
    keep[...] = here[pl.ds(stay, half), :] + came[pl.ds(stay, half), :].astype(F32)


def text_kernel(scal, here, came, out):
    half = COLS // 2
    loss = scal[0:8, :] + value(came[half : half + TAIL, 0:LANES])
    both = (here[...] + came[0:half, :].astype(F32)).astype(BF16)
    tile = pieces(loss[0:1])
    for z in range(N_Z):
        for k in range(SLABS):
            out[z, k * EACH : (k + 1) * EACH, :] = both[z * EACH : (z + 1) * EACH, k * LANES : (k + 1) * LANES]
        out[z, SLABS * EACH :, :] = tile


def pack_kernel(total, keep, got, pack, out):
    half = ROWS // 4
    out[...] = total[...] + value(got[half : half + TAIL, 0:LANES])
    pack[...] = (keep[...] + got[0:half, :].astype(F32)).astype(BF16).reshape(N_Y, EACH, WIDTH)


def image_kernel(got, out):
    acc = got[0].astype(F32)
    for n in range(1, N_Y):
        acc = acc + got[n].astype(F32)
    out[...] = acc.reshape(EACH, 1, WIDTH)


def final_kernel(got, total, out, loss):
    acc = got[0].astype(F32)
    for z in range(1, N_Z):
        acc = acc + got[z].astype(F32)
    row = acc[SLABS * EACH :]
    acc = jnp.concatenate([acc[k * EACH : (k + 1) * EACH] for k in range(SLABS)], axis=1)
    out[...] = acc.reshape(EACH, 1, WIDTH)
    whole = jnp.sum(jnp.where(lanes((1, LANES)) < 3, row[0:1], 0.0))
    loss[0, 0] = (jnp.max(total[...]) + whole) / (2.0 * PAIRS)


def body(image_emb, text_emb, logit_scale):
    places = [lax.axis_index(a) for a in ("z", "c", "y", "xh", "xl")]
    idx = jnp.stack(places).astype(jnp.int32)
    (spread,) = call(spread_kernel, [((N_COL, EACH, WIDTH), BF16)], [], image_emb.reshape(EACH, WIDTH))
    images = exchange(spread, ("xl", "xh", "y")).reshape(ROWS, WIDTH)
    texts = lax.all_gather(text_emb.reshape(EACH, WIDTH), "c")
    texts = lax.all_gather(texts, "z").reshape(COLS, WIDTH)
    scores, cpack, rpack = call(
        score_kernel,
        [((ROWS, COLS), F32), ((N_ROW, 8, LANES), F32), ((8, LANES), F32)],
        [],
        idx, logit_scale, images, texts,
    )
    col_got = exchange(cpack, ("z", "c"))
    near = lax.all_gather(rpack, ("xl", "xh"))
    col_lse, ypack = call(merge_kernel, [((8, COLS), F32), ((N_Y, 8, LANES), F32)], [], col_got, near)
    row_got = exchange(ypack, "y")
    iaway, taway, there, scal, delta = call(
        grad_kernel,
        [
            ((ROWS // 2 + TAIL, WIDTH), BF16),
            ((COLS // 2 + TAIL, WIDTH), BF16),
            ((COLS // 2, WIDTH), F32),
            ((16, LANES), F32),
            ((N_XL, ROWS // 2, COLS), BF16),
        ],
        [((N_Z, N_C, EACH, WIDTH), F32)],
        idx, logit_scale, scores, images, texts, row_got, col_lse,
    )
    tcame = shift(taway, "c", 1)
    icame = shift(iaway, "xl", 1)
    (ihere,) = call(keep_kernel, [((ROWS // 2, WIDTH), F32)], [], idx, delta, texts)
    xaway, keep, total = call(
        across_kernel,
        [((ROWS // 4 + TAIL, WIDTH), BF16), ((ROWS // 4, WIDTH), F32), ((8, LANES), F32)],
        [],
        idx, scal, ihere, icame,
    )
    xcame = shift(xaway, "xh", 1)
    (tpack,) = call(text_kernel, [((N_Z, SLABS * EACH + TAIL, LANES), BF16)], [], scal, there, tcame)
    text_got = exchange(tpack, "z")
    ypack, total = call(pack_kernel, [((N_Y, EACH, WIDTH), BF16), ((8, LANES), F32)], [], total, keep, xcame)
    image_got = exchange(ypack, "y")
    (image_grad,) = call(image_kernel, [((EACH, 1, WIDTH), F32)], [], image_got)
    text_grad, loss = call(final_kernel, [((EACH, 1, WIDTH), F32), ((1, 1), F32)], [], text_got, total)
    return loss[0, 0], image_grad, text_grad


def solution(mesh):
    fine = Mesh(mesh.devices.reshape(N_XL, N_Z, N_Y, N_XH, N_C), ROW + COL)
    placed = (P(ROW, COL, None), P(COL, ROW, None), P())
    return jax.shard_map(
        body,
        mesh=fine,
        in_specs=placed,
        out_specs=(P(), P(ROW, COL, None), P(COL, ROW, None)),
        check_vma=False,
    )
```

```python
import functools

import jax
import jax.numpy as jnp
from jax import lax
from jax.experimental import pallas as pl
from jax.experimental.pallas import tpu as pltpu
from jax.sharding import Mesh, PartitionSpec as P


COL = ("y", "xh", "c")
ROW = ("xl", "z")
N_XL, N_Z, N_Y, N_XH, N_C = 2, 12, 8, 2, 2
N_ROW, N_COL = N_XL * N_Z, N_Y * N_XH * N_C
EACH = 16
WIDTH = 1024
ROWS, COLS = EACH * N_COL, EACH * N_ROW
PAIRS = ROWS * N_ROW
LANES = 128
TAIL = 8
SLABS = WIDTH // LANES
BF16 = jnp.bfloat16
F32 = jnp.float32
VMEM = pl.BlockSpec(memory_space=pltpu.VMEM)
SMEM = pl.BlockSpec(memory_space=pltpu.SMEM)


def exchange(x, axes):
    return lax.all_to_all(x, axes, 0, 0, tiled=False)


def shift(x, axis, k):
    n = lax.axis_size(axis)
    return lax.ppermute(x, axis, [(i, (i + k) % n) for i in range(n)])


def call(kernel, outs, scratch, *args):
    in_specs = [SMEM if a.ndim == 1 else VMEM for a in args]
    return pl.pallas_call(
        kernel,
        out_shape=[jax.ShapeDtypeStruct(s, d) for s, d in outs],
        in_specs=in_specs,
        out_specs=[SMEM if s == (1, 1) else VMEM for s, _ in outs],
        scratch_shapes=[pltpu.VMEM(s, d) for s, d in scratch],
        compiler_params=pltpu.CompilerParams(vmem_limit_bytes=24 << 20),
    )(*args)


def lanes(shape):
    return lax.broadcasted_iota(jnp.int32, shape, 1)


def merged(parts):
    peak = functools.reduce(jnp.maximum, parts)
    return peak + jnp.log(sum(jnp.exp(p - peak) for p in parts))


def pieces(v):
    v = jnp.broadcast_to(v, (TAIL, LANES))
    hi = v.astype(BF16).astype(F32)
    mid = (v - hi).astype(BF16).astype(F32)
    low = v - hi - mid
    at = lanes((TAIL, LANES))
    return jnp.where(at == 0, hi, jnp.where(at == 1, mid, jnp.where(at == 2, low, 0.0))).astype(BF16)


def value(tile):
    row = tile.astype(F32)[0:1]
    return jnp.sum(jnp.where(lanes((1, LANES)) < 3, row, 0.0))


def put_tail(ref, at, v):
    ref[at : at + TAIL, :] = jnp.zeros((TAIL, WIDTH), BF16)
    ref[at : at + TAIL, 0:LANES] = pieces(v)


def diagonal(idx, start, count):
    i = lax.broadcasted_iota(jnp.int32, (count, COLS), 0) + start
    j = lax.broadcasted_iota(jnp.int32, (count, COLS), 1)
    i_dev = ((i >> 4) & 7) * (N_XH * N_C) + ((i >> 7) & 1) * N_C + (i >> 8)
    j_dev = ((j >> 4) & 1) * N_Z + (j >> 5)
    row_ids = (EACH * idx[0] + (i & 15)) * N_COL + i_dev
    col_ids = (EACH * idx[1] + (j & 15)) * N_ROW + j_dev
    return row_ids == col_ids


def spread_kernel(block, out):
    tile = block[...]
    for n in range(N_COL):
        out[n] = tile


def score_kernel(idx, fac, im, tx, sc, cpack, rpack):
    s = fac[0] * lax.dot_general(im[...], tx[...], (((1,), (1,)), ((), ())), preferred_element_type=F32)
    sc[...] = s
    peak = jnp.max(s, axis=0, keepdims=True)
    col = peak + jnp.log(jnp.sum(jnp.exp(s - peak), axis=0, keepdims=True))
    for k in range(COLS // LANES):
        tile = jnp.broadcast_to(col[:, k * LANES : (k + 1) * LANES], (N_ROW, LANES))
        for n in range(N_ROW):
            cpack[n, k : k + 1, :] = tile[n : n + 1]
    peak = jnp.max(s, axis=1, keepdims=True)
    row = peak + jnp.log(jnp.sum(jnp.exp(s - peak), axis=1, keepdims=True))
    for k in range(ROWS // LANES):
        tile = jnp.broadcast_to(row[k * LANES : (k + 1) * LANES], (LANES, LANES))
        rpack[k : k + 1, :] = tile.T[0:1]
    diag = jnp.sum(jnp.where(diagonal(idx, 0, ROWS), s, 0.0))
    rpack[4:5, :] = jnp.full((1, LANES), diag)


def merge_kernel(col, near, clse, pack):
    lse = merged([col[n] for n in range(N_ROW)])
    total = jnp.zeros((1, LANES), F32)
    for k in range(COLS // LANES):
        clse[:, k * LANES : (k + 1) * LANES] = jnp.broadcast_to(lse[k : k + 1], (8, LANES))
        total = total + lse[k : k + 1]
    total = jnp.full((1, LANES), jnp.sum(total))
    rows = merged([near[n] for n in range(N_XH * N_C)])
    diag = sum(near[n, 4:5, :] for n in range(N_XH * N_C))
    for n in range(N_Y):
        pack[n, 0:4, :] = rows[0:4]
        pack[n, 4:5, :] = diag
        pack[n, 5:6, :] = total


def grad_kernel(idx, fac, sc, im, tx, got, clse, iaway, taway, there, scal, ihere, delta, part):
    rows = merged([got[n] for n in range(N_Y)])[0:4]
    diag = sum(got[n, 4:5, :] for n in range(N_Y))
    total = sum(got[n, 5:6, :] for n in range(N_Y))
    row_loss = jnp.full((1, LANES), jnp.sum(rows)) - 2.0 * diag
    scal[0:8, :] = jnp.broadcast_to(row_loss, (8, LANES))
    scal[8:16, :] = jnp.broadcast_to(total, (8, LANES))
    c, xl = idx[2], idx[5]
    col = clse[0:1, :]
    for k in range(ROWS // LANES):
        s = sc[k * LANES : (k + 1) * LANES, :]
        tile = jnp.broadcast_to(rows[k : k + 1], (LANES, LANES)).T
        lse = jnp.concatenate([tile] * (COLS // LANES), axis=1)
        eye = diagonal(idx, k * LANES, LANES)
        d = jnp.exp(s - lse) + jnp.exp(s - col) - jnp.where(eye, 2.0, 0.0)
        delta[k // 2, (k % 2) * LANES : (k % 2 + 1) * LANES, :] = (fac[0] * d).astype(BF16)
    iaway[0 : ROWS // 2, :] = jnp.dot(delta[1 - c], tx[...], preferred_element_type=F32).astype(BF16)
    put_tail(iaway, ROWS // 2, total)
    whole = delta[...].reshape(ROWS, COLS)
    part[...] = lax.dot_general(
        whole, im[...], (((0,), (0,)), ((), ())), preferred_element_type=F32
    ).reshape(N_Z, N_XL, EACH, WIDTH)
    for z in range(N_Z):
        taway[z * EACH : (z + 1) * EACH, :] = part[z, 1 - xl].astype(BF16)
        there[z * EACH : (z + 1) * EACH, :] = part[z, xl]
    put_tail(taway, COLS // 2, row_loss)
    ihere[...] = jnp.dot(delta[c], tx[...], preferred_element_type=F32)


def across_kernel(idx, scal, here, came, away, keep, out):
    half = ROWS // 4
    xh = idx[3]
    go = pl.multiple_of((1 - xh) * half, half)
    stay = pl.multiple_of(xh * half, half)
    total = scal[8:16, :] + value(came[ROWS // 2 : ROWS // 2 + TAIL, 0:LANES])
    out[...] = total
    away[0:half, :] = (here[pl.ds(go, half), :] + came[pl.ds(go, half), :].astype(F32)).astype(BF16)
    put_tail(away, half, total[0:1])
    keep[...] = here[pl.ds(stay, half), :] + came[pl.ds(stay, half), :].astype(F32)


def text_kernel(scal, here, came, out):
    half = COLS // 2
    loss = scal[0:8, :] + value(came[half : half + TAIL, 0:LANES])
    both = (here[...] + came[0:half, :].astype(F32)).astype(BF16)
    tile = pieces(loss[0:1])
    for z in range(N_Z):
        for k in range(SLABS):
            out[z, k * EACH : (k + 1) * EACH, :] = both[z * EACH : (z + 1) * EACH, k * LANES : (k + 1) * LANES]
        out[z, SLABS * EACH :, :] = tile


def ring_kernel(idx, total, keep, got, ahead, behind, near, out):
    y = idx[4]
    half = ROWS // 4
    out[...] = total[...] + value(got[half : half + TAIL, 0:LANES])

    def block(k):
        at = pl.multiple_of(((y + k) & (N_Y - 1)) * EACH, EACH)
        return keep[pl.ds(at, EACH), :] + got[pl.ds(at, EACH), :].astype(F32)

    for n, k in enumerate((1, 4, 6)):
        ahead[n * EACH : (n + 1) * EACH, :] = block(k).astype(BF16)
    for n, k in enumerate((7, 2)):
        behind[n * EACH : (n + 1) * EACH, :] = block(k).astype(BF16)
    for n, k in enumerate((0, 3, 5)):
        near[n * EACH : (n + 1) * EACH, :] = block(k)


def side_kernel(near, low, high, up, down, mid):
    e = EACH
    mid[...] = near[0:e, :] + low[0:e, :].astype(F32) + high[0:e, :].astype(F32)
    up[...] = (near[e : 2 * e, :] + low[e : 2 * e, :].astype(F32) + high[e:, :].astype(F32)).astype(BF16)
    down[...] = (near[2 * e :, :] + low[2 * e :, :].astype(F32)).astype(BF16)


def image_kernel(mid, left, right, out):
    out[...] = (mid[...] + left[...].astype(F32) + right[...].astype(F32)).reshape(EACH, 1, WIDTH)


def final_kernel(got, total, out, loss):
    acc = got[0].astype(F32)
    for z in range(1, N_Z):
        acc = acc + got[z].astype(F32)
    row = acc[SLABS * EACH :]
    acc = jnp.concatenate([acc[k * EACH : (k + 1) * EACH] for k in range(SLABS)], axis=1)
    out[...] = acc.reshape(EACH, 1, WIDTH)
    whole = jnp.sum(jnp.where(lanes((1, LANES)) < 3, row[0:1], 0.0))
    loss[0, 0] = (jnp.max(total[...]) + whole) / (2.0 * PAIRS)


def body(image_emb, text_emb, logit_scale):
    places = [lax.axis_index(a) for a in (ROW, COL, "c", "xh", "y", "xl")]
    idx = jnp.stack(places).astype(jnp.int32)
    (spread,) = call(spread_kernel, [((N_COL, EACH, WIDTH), BF16)], [], image_emb.reshape(EACH, WIDTH))
    images = exchange(spread, ("c", "xh", "y")).reshape(ROWS, WIDTH)
    texts = lax.all_gather(text_emb.reshape(EACH, WIDTH), "xl")
    texts = lax.all_gather(texts, "z").reshape(COLS, WIDTH)
    scores, cpack, rpack = call(
        score_kernel,
        [((ROWS, COLS), F32), ((N_ROW, 8, LANES), F32), ((8, LANES), F32)],
        [],
        idx, logit_scale, images, texts,
    )
    col_got = exchange(cpack, ROW)
    near = lax.all_gather(rpack, ("xh", "c"))
    col_lse, ypack = call(merge_kernel, [((8, COLS), F32), ((N_Y, 8, LANES), F32)], [], col_got, near)
    row_got = exchange(ypack, "y")
    iaway, taway, there, scal, ihere = call(
        grad_kernel,
        [
            ((ROWS // 2 + TAIL, WIDTH), BF16),
            ((COLS // 2 + TAIL, WIDTH), BF16),
            ((COLS // 2, WIDTH), F32),
            ((16, LANES), F32),
            ((ROWS // 2, WIDTH), F32),
        ],
        [((N_C, ROWS // 2, COLS), BF16), ((N_Z, N_XL, EACH, WIDTH), F32)],
        idx, logit_scale, scores, images, texts, row_got, col_lse,
    )
    tcame = shift(taway, "xl", 1)
    icame = shift(iaway, "c", 1)
    xaway, keep, total = call(
        across_kernel,
        [((ROWS // 4 + TAIL, WIDTH), BF16), ((ROWS // 4, WIDTH), F32), ((8, LANES), F32)],
        [],
        idx, scal, ihere, icame,
    )
    xcame = shift(xaway, "xh", 1)
    (tpack,) = call(text_kernel, [((N_Z, SLABS * EACH + TAIL, LANES), BF16)], [], scal, there, tcame)
    text_got = exchange(tpack, "z")
    ahead, behind, near3, total = call(
        ring_kernel,
        [((3 * EACH, WIDTH), BF16), ((2 * EACH, WIDTH), BF16), ((3 * EACH, WIDTH), F32), ((8, LANES), F32)],
        [],
        idx, total, keep, xcame,
    )
    low = shift(ahead, "y", 1)
    high = shift(behind, "y", 7)
    up, down, mid = call(
        side_kernel,
        [((EACH, WIDTH), BF16), ((EACH, WIDTH), BF16), ((EACH, WIDTH), F32)],
        [],
        near3, low, high,
    )
    left = shift(up, "y", 3)
    right = shift(down, "y", 5)
    text_grad, loss = call(final_kernel, [((EACH, 1, WIDTH), F32), ((1, 1), F32)], [], text_got, total)
    (image_grad,) = call(image_kernel, [((EACH, 1, WIDTH), F32)], [], mid, left, right)
    return loss[0, 0], image_grad, text_grad


def solution(mesh):
    fine = Mesh(mesh.devices.reshape(N_XL, N_Z, N_Y, N_XH, N_C), ROW + COL)
    placed = (P(ROW, COL, None), P(COL, ROW, None), P())
    return jax.shard_map(
        body,
        mesh=fine,
        in_specs=placed,
        out_specs=(P(), P(ROW, COL, None), P(COL, ROW, None)),
        check_vma=False,
    )
```

```python
import functools

import jax
import jax.numpy as jnp
from jax import lax
from jax.experimental import pallas as pl
from jax.experimental.pallas import tpu as pltpu
from jax.sharding import Mesh, PartitionSpec as P


COL = ("y", "xh", "c")
ROW = ("xl", "z")
N_XL, N_Z, N_Y, N_XH, N_C = 2, 12, 8, 2, 2
N_ROW, N_COL = N_XL * N_Z, N_Y * N_XH * N_C
EACH = 16
WIDTH = 1024
ROWS, COLS = EACH * N_COL, EACH * N_ROW
PAIRS = ROWS * N_ROW
LANES = 128
TAIL = 8
SLABS = WIDTH // LANES
BF16 = jnp.bfloat16
F32 = jnp.float32
VMEM = pl.BlockSpec(memory_space=pltpu.VMEM)
SMEM = pl.BlockSpec(memory_space=pltpu.SMEM)


def exchange(x, axes):
    return lax.all_to_all(x, axes, 0, 0, tiled=False)


def shift(x, axis, k):
    n = lax.axis_size(axis)
    return lax.ppermute(x, axis, [(i, (i + k) % n) for i in range(n)])


def call(kernel, outs, scratch, *args):
    in_specs = [SMEM if a.ndim == 1 else VMEM for a in args]
    return pl.pallas_call(
        kernel,
        out_shape=[jax.ShapeDtypeStruct(s, d) for s, d in outs],
        in_specs=in_specs,
        out_specs=[SMEM if s == (1, 1) else VMEM for s, _ in outs],
        scratch_shapes=[pltpu.VMEM(s, d) for s, d in scratch],
        compiler_params=pltpu.CompilerParams(vmem_limit_bytes=24 << 20),
    )(*args)


def lanes(shape):
    return lax.broadcasted_iota(jnp.int32, shape, 1)


def merged(parts):
    peak = functools.reduce(jnp.maximum, parts)
    return peak + jnp.log(sum(jnp.exp(p - peak) for p in parts))


def pieces(v):
    v = jnp.broadcast_to(v, (TAIL, LANES))
    hi = v.astype(BF16).astype(F32)
    mid = (v - hi).astype(BF16).astype(F32)
    low = v - hi - mid
    at = lanes((TAIL, LANES))
    return jnp.where(at == 0, hi, jnp.where(at == 1, mid, jnp.where(at == 2, low, 0.0))).astype(BF16)


def value(tile):
    row = tile.astype(F32)[0:1]
    return jnp.sum(jnp.where(lanes((1, LANES)) < 3, row, 0.0))


def put_tail(ref, at, v):
    ref[at : at + TAIL, :] = jnp.zeros((TAIL, WIDTH), BF16)
    ref[at : at + TAIL, 0:LANES] = pieces(v)


def diagonal(idx, start, count):
    i = lax.broadcasted_iota(jnp.int32, (count, COLS), 0) + start
    j = lax.broadcasted_iota(jnp.int32, (count, COLS), 1)
    i_dev = ((i >> 4) & 7) * (N_XH * N_C) + ((i >> 7) & 1) * N_C + (i >> 8)
    j_dev = ((j >> 4) & 1) * N_Z + (j >> 5)
    row_ids = (EACH * idx[0] + (i & 15)) * N_COL + i_dev
    col_ids = (EACH * idx[1] + (j & 15)) * N_ROW + j_dev
    return row_ids == col_ids


def spread_kernel(block, out):
    tile = block[...]
    for n in range(N_COL):
        out[n] = tile


def stack_kernel(idx, own, came, out):
    xl = idx[5]
    out[xl] = own[...]
    out[1 - xl] = came[...]


def score_kernel(idx, fac, im, tx, sc, cpack, rpack):
    s = fac[0] * lax.dot_general(im[...], tx[...], (((1,), (1,)), ((), ())), preferred_element_type=F32)
    sc[...] = s
    peak = jnp.max(s, axis=0, keepdims=True)
    col = peak + jnp.log(jnp.sum(jnp.exp(s - peak), axis=0, keepdims=True))
    for k in range(COLS // LANES):
        tile = jnp.broadcast_to(col[:, k * LANES : (k + 1) * LANES], (N_ROW, LANES))
        for n in range(N_ROW):
            cpack[n, k : k + 1, :] = tile[n : n + 1]
    peak = jnp.max(s, axis=1, keepdims=True)
    row = peak + jnp.log(jnp.sum(jnp.exp(s - peak), axis=1, keepdims=True))
    for k in range(ROWS // LANES):
        tile = jnp.broadcast_to(row[k * LANES : (k + 1) * LANES], (LANES, LANES))
        rpack[k : k + 1, :] = tile.T[0:1]
    diag = jnp.sum(jnp.where(diagonal(idx, 0, ROWS), s, 0.0))
    rpack[4:5, :] = jnp.full((1, LANES), diag)


def merge_kernel(col, near, clse, pack):
    lse = merged([col[n] for n in range(N_ROW)])
    total = jnp.zeros((1, LANES), F32)
    for k in range(COLS // LANES):
        clse[:, k * LANES : (k + 1) * LANES] = jnp.broadcast_to(lse[k : k + 1], (8, LANES))
        total = total + lse[k : k + 1]
    total = jnp.full((1, LANES), jnp.sum(total))
    rows = merged([near[n] for n in range(N_XH * N_C)])
    diag = sum(near[n, 4:5, :] for n in range(N_XH * N_C))
    for n in range(N_Y):
        pack[n, 0:4, :] = rows[0:4]
        pack[n, 4:5, :] = diag
        pack[n, 5:6, :] = total


def grad_kernel(idx, fac, sc, im, tx, got, clse, iaway, taway, there, scal, delta, part):
    rows = merged([got[n] for n in range(N_Y)])[0:4]
    diag = sum(got[n, 4:5, :] for n in range(N_Y))
    total = sum(got[n, 5:6, :] for n in range(N_Y))
    row_loss = jnp.full((1, LANES), jnp.sum(rows)) - 2.0 * diag
    scal[0:8, :] = jnp.broadcast_to(row_loss, (8, LANES))
    scal[8:16, :] = jnp.broadcast_to(total, (8, LANES))
    c, xl = idx[2], idx[5]
    col = clse[0:1, :]
    for k in range(ROWS // LANES):
        s = sc[k * LANES : (k + 1) * LANES, :]
        tile = jnp.broadcast_to(rows[k : k + 1], (LANES, LANES)).T
        lse = jnp.concatenate([tile] * (COLS // LANES), axis=1)
        eye = diagonal(idx, k * LANES, LANES)
        d = jnp.exp(s - lse) + jnp.exp(s - col) - jnp.where(eye, 2.0, 0.0)
        delta[k // 2, (k % 2) * LANES : (k % 2 + 1) * LANES, :] = (fac[0] * d).astype(BF16)
    iaway[0 : ROWS // 2, :] = jnp.dot(delta[1 - c], tx[...], preferred_element_type=F32).astype(BF16)
    put_tail(iaway, ROWS // 2, total)
    whole = delta[...].reshape(ROWS, COLS)
    part[...] = lax.dot_general(
        whole, im[...], (((0,), (0,)), ((), ())), preferred_element_type=F32
    ).reshape(N_Z, N_XL, EACH, WIDTH)
    for z in range(N_Z):
        taway[z * EACH : (z + 1) * EACH, :] = part[z, 1 - xl].astype(BF16)
        there[z * EACH : (z + 1) * EACH, :] = part[z, xl]
    put_tail(taway, COLS // 2, row_loss)


def keep_kernel(idx, delta, tx, ihere):
    ihere[...] = jnp.dot(delta[idx[2]], tx[...], preferred_element_type=F32)


def across_kernel(idx, scal, here, came, away, keep, out):
    half = ROWS // 4
    xh = idx[3]
    go = pl.multiple_of((1 - xh) * half, half)
    stay = pl.multiple_of(xh * half, half)
    total = scal[8:16, :] + value(came[ROWS // 2 : ROWS // 2 + TAIL, 0:LANES])
    out[...] = total
    away[0:half, :] = (here[pl.ds(go, half), :] + came[pl.ds(go, half), :].astype(F32)).astype(BF16)
    put_tail(away, half, total[0:1])
    keep[...] = here[pl.ds(stay, half), :] + came[pl.ds(stay, half), :].astype(F32)


def text_kernel(scal, here, came, out):
    half = COLS // 2
    loss = scal[0:8, :] + value(came[half : half + TAIL, 0:LANES])
    both = (here[...] + came[0:half, :].astype(F32)).astype(BF16)
    tile = pieces(loss[0:1])
    for z in range(N_Z):
        for k in range(SLABS):
            out[z, k * EACH : (k + 1) * EACH, :] = both[z * EACH : (z + 1) * EACH, k * LANES : (k + 1) * LANES]
        out[z, SLABS * EACH :, :] = tile


def ring_kernel(idx, total, keep, got, ahead, behind, near, out):
    y = idx[4]
    half = ROWS // 4
    out[...] = total[...] + value(got[half : half + TAIL, 0:LANES])

    def block(k):
        at = pl.multiple_of(((y + k) & (N_Y - 1)) * EACH, EACH)
        return keep[pl.ds(at, EACH), :] + got[pl.ds(at, EACH), :].astype(F32)

    for n, k in enumerate((1, 4, 6)):
        ahead[n * EACH : (n + 1) * EACH, :] = block(k).astype(BF16)
    for n, k in enumerate((7, 2)):
        behind[n * EACH : (n + 1) * EACH, :] = block(k).astype(BF16)
    for n, k in enumerate((0, 3, 5)):
        near[n * EACH : (n + 1) * EACH, :] = block(k)


def side_kernel(near, low, high, up, down, mid):
    e = EACH
    mid[...] = near[0:e, :] + low[0:e, :].astype(F32) + high[0:e, :].astype(F32)
    up[...] = (near[e : 2 * e, :] + low[e : 2 * e, :].astype(F32) + high[e:, :].astype(F32)).astype(BF16)
    down[...] = (near[2 * e :, :] + low[2 * e :, :].astype(F32)).astype(BF16)


def image_kernel(mid, left, right, out):
    out[...] = (mid[...] + left[...].astype(F32) + right[...].astype(F32)).reshape(EACH, 1, WIDTH)


def final_kernel(got, total, out, loss):
    acc = got[0].astype(F32)
    for z in range(1, N_Z):
        acc = acc + got[z].astype(F32)
    row = acc[SLABS * EACH :]
    acc = jnp.concatenate([acc[k * EACH : (k + 1) * EACH] for k in range(SLABS)], axis=1)
    out[...] = acc.reshape(EACH, 1, WIDTH)
    whole = jnp.sum(jnp.where(lanes((1, LANES)) < 3, row[0:1], 0.0))
    loss[0, 0] = (jnp.max(total[...]) + whole) / (2.0 * PAIRS)


def body(image_emb, text_emb, logit_scale):
    places = [lax.axis_index(a) for a in (ROW, COL, "c", "xh", "y", "xl")]
    idx = jnp.stack(places).astype(jnp.int32)
    (spread,) = call(spread_kernel, [((N_COL, EACH, WIDTH), BF16)], [], image_emb.reshape(EACH, WIDTH))
    images = exchange(spread, ("c", "xh", "y")).reshape(ROWS, WIDTH)
    own = text_emb.reshape(EACH, WIDTH)
    came = shift(own, "xl", 1)
    (texts,) = call(stack_kernel, [((N_XL, EACH, WIDTH), BF16)], [], idx, own, came)
    texts = lax.all_gather(texts, "z").reshape(COLS, WIDTH)
    scores, cpack, rpack = call(
        score_kernel,
        [((ROWS, COLS), F32), ((N_ROW, 8, LANES), F32), ((8, LANES), F32)],
        [],
        idx, logit_scale, images, texts,
    )
    col_got = exchange(cpack, ROW)
    near = lax.all_gather(rpack, ("xh", "c"))
    col_lse, ypack = call(merge_kernel, [((8, COLS), F32), ((N_Y, 8, LANES), F32)], [], col_got, near)
    row_got = exchange(ypack, "y")
    iaway, taway, there, scal, delta = call(
        grad_kernel,
        [
            ((ROWS // 2 + TAIL, WIDTH), BF16),
            ((COLS // 2 + TAIL, WIDTH), BF16),
            ((COLS // 2, WIDTH), F32),
            ((16, LANES), F32),
            ((N_C, ROWS // 2, COLS), BF16),
        ],
        [((N_Z, N_XL, EACH, WIDTH), F32)],
        idx, logit_scale, scores, images, texts, row_got, col_lse,
    )
    tcame = shift(taway, "xl", 1)
    icame = shift(iaway, "c", 1)
    (ihere,) = call(keep_kernel, [((ROWS // 2, WIDTH), F32)], [], idx, delta, texts)
    xaway, keep, total = call(
        across_kernel,
        [((ROWS // 4 + TAIL, WIDTH), BF16), ((ROWS // 4, WIDTH), F32), ((8, LANES), F32)],
        [],
        idx, scal, ihere, icame,
    )
    xcame = shift(xaway, "xh", 1)
    (tpack,) = call(text_kernel, [((N_Z, SLABS * EACH + TAIL, LANES), BF16)], [], scal, there, tcame)
    text_got = exchange(tpack, "z")
    ahead, behind, near3, total = call(
        ring_kernel,
        [((3 * EACH, WIDTH), BF16), ((2 * EACH, WIDTH), BF16), ((3 * EACH, WIDTH), F32), ((8, LANES), F32)],
        [],
        idx, total, keep, xcame,
    )
    low = shift(ahead, "y", 1)
    high = shift(behind, "y", 7)
    up, down, mid = call(
        side_kernel,
        [((EACH, WIDTH), BF16), ((EACH, WIDTH), BF16), ((EACH, WIDTH), F32)],
        [],
        near3, low, high,
    )
    left = shift(up, "y", 3)
    right = shift(down, "y", 5)
    text_grad, loss = call(final_kernel, [((EACH, 1, WIDTH), F32), ((1, 1), F32)], [], text_got, total)
    (image_grad,) = call(image_kernel, [((EACH, 1, WIDTH), F32)], [], mid, left, right)
    return loss[0, 0], image_grad, text_grad


def solution(mesh):
    fine = Mesh(mesh.devices.reshape(N_XL, N_Z, N_Y, N_XH, N_C), ROW + COL)
    placed = (P(ROW, COL, None), P(COL, ROW, None), P())
    return jax.shard_map(
        body,
        mesh=fine,
        in_specs=placed,
        out_specs=(P(), P(ROW, COL, None), P(COL, ROW, None)),
        check_vma=False,
    )
```

```python
import functools

import jax
import jax.numpy as jnp
from jax import lax
from jax.experimental import pallas as pl
from jax.experimental.pallas import tpu as pltpu
from jax.sharding import Mesh, PartitionSpec as P


COL = ("y", "xh", "c")
ROW = ("xl", "z")
N_XL, N_Z, N_Y, N_XH, N_C = 2, 12, 8, 2, 2
N_ROW, N_COL = N_XL * N_Z, N_Y * N_XH * N_C
EACH = 16
WIDTH = 1024
ROWS, COLS = EACH * N_COL, EACH * N_ROW
PAIRS = ROWS * N_ROW
LANES = 128
TAIL = 8
SLABS = WIDTH // LANES
BF16 = jnp.bfloat16
F32 = jnp.float32
VMEM = pl.BlockSpec(memory_space=pltpu.VMEM)
SMEM = pl.BlockSpec(memory_space=pltpu.SMEM)


def exchange(x, axes):
    return lax.all_to_all(x, axes, 0, 0, tiled=False)


def shift(x, axis, k):
    n = lax.axis_size(axis)
    return lax.ppermute(x, axis, [(i, (i + k) % n) for i in range(n)])


def call(kernel, outs, scratch, *args):
    in_specs = [SMEM if a.ndim == 1 else VMEM for a in args]
    return pl.pallas_call(
        kernel,
        out_shape=[jax.ShapeDtypeStruct(s, d) for s, d in outs],
        in_specs=in_specs,
        out_specs=[SMEM if s == (1, 1) else VMEM for s, _ in outs],
        scratch_shapes=[pltpu.VMEM(s, d) for s, d in scratch],
        compiler_params=pltpu.CompilerParams(vmem_limit_bytes=24 << 20),
    )(*args)


def lanes(shape):
    return lax.broadcasted_iota(jnp.int32, shape, 1)


def merged(parts):
    peak = functools.reduce(jnp.maximum, parts)
    return peak + jnp.log(sum(jnp.exp(p - peak) for p in parts))


def pieces(v):
    v = jnp.broadcast_to(v, (TAIL, LANES))
    hi = v.astype(BF16).astype(F32)
    mid = (v - hi).astype(BF16).astype(F32)
    low = v - hi - mid
    at = lanes((TAIL, LANES))
    return jnp.where(at == 0, hi, jnp.where(at == 1, mid, jnp.where(at == 2, low, 0.0))).astype(BF16)


def value(tile):
    row = tile.astype(F32)[0:1]
    return jnp.sum(jnp.where(lanes((1, LANES)) < 3, row, 0.0))


def put_tail(ref, at, v):
    ref[at : at + TAIL, :] = jnp.zeros((TAIL, WIDTH), BF16)
    ref[at : at + TAIL, 0:LANES] = pieces(v)


def diagonal(idx, start, count):
    i = lax.broadcasted_iota(jnp.int32, (count, COLS), 0) + start
    j = lax.broadcasted_iota(jnp.int32, (count, COLS), 1)
    i_dev = ((i >> 4) & 7) * (N_XH * N_C) + ((i >> 7) & 1) * N_C + (i >> 8)
    j_dev = ((j >> 4) & 1) * N_Z + (j >> 5)
    row_ids = (EACH * idx[0] + (i & 15)) * N_COL + i_dev
    col_ids = (EACH * idx[1] + (j & 15)) * N_ROW + j_dev
    return row_ids == col_ids


def spread_kernel(idx, block, out):
    tile = block[...]
    for n in range(N_COL):
        out[n] = tile


def stack_kernel(idx, own, came, out):
    xl = idx[5]
    out[xl] = own[...]
    out[1 - xl] = came[...]


def score_kernel(fac, im, tx, sc, cpack):
    s = fac[0] * lax.dot_general(im[...], tx[...], (((1,), (1,)), ((), ())), preferred_element_type=F32)
    sc[...] = s
    peak = jnp.max(s, axis=0, keepdims=True)
    col = peak + jnp.log(jnp.sum(jnp.exp(s - peak), axis=0, keepdims=True))
    for k in range(COLS // LANES):
        tile = jnp.broadcast_to(col[:, k * LANES : (k + 1) * LANES], (N_ROW, LANES))
        for n in range(N_ROW):
            cpack[n, k : k + 1, :] = tile[n : n + 1]


def row_kernel(idx, sc, rpack):
    s = sc[...]
    peak = jnp.max(s, axis=1, keepdims=True)
    row = peak + jnp.log(jnp.sum(jnp.exp(s - peak), axis=1, keepdims=True))
    for k in range(ROWS // LANES):
        tile = jnp.broadcast_to(row[k * LANES : (k + 1) * LANES], (LANES, LANES))
        rpack[k : k + 1, :] = tile.T[0:1]
    diag = jnp.sum(jnp.where(diagonal(idx, 0, ROWS), s, 0.0))
    rpack[4:5, :] = jnp.full((1, LANES), diag)


def merge_kernel(col, near, clse, pack):
    lse = merged([col[n] for n in range(N_ROW)])
    total = jnp.zeros((1, LANES), F32)
    for k in range(COLS // LANES):
        clse[:, k * LANES : (k + 1) * LANES] = jnp.broadcast_to(lse[k : k + 1], (8, LANES))
        total = total + lse[k : k + 1]
    total = jnp.full((1, LANES), jnp.sum(total))
    rows = merged([near[n] for n in range(N_XH * N_C)])
    diag = sum(near[n, 4:5, :] for n in range(N_XH * N_C))
    for n in range(N_Y):
        pack[n, 0:4, :] = rows[0:4]
        pack[n, 4:5, :] = diag
        pack[n, 5:6, :] = total


def grad_kernel(idx, fac, sc, im, tx, got, clse, iaway, taway, there, scal, delta, part):
    rows = merged([got[n] for n in range(N_Y)])[0:4]
    diag = sum(got[n, 4:5, :] for n in range(N_Y))
    total = sum(got[n, 5:6, :] for n in range(N_Y))
    row_loss = jnp.full((1, LANES), jnp.sum(rows)) - 2.0 * diag
    scal[0:8, :] = jnp.broadcast_to(row_loss, (8, LANES))
    scal[8:16, :] = jnp.broadcast_to(total, (8, LANES))
    c, xl = idx[2], idx[5]
    col = clse[0:1, :]
    for k in range(ROWS // LANES):
        s = sc[k * LANES : (k + 1) * LANES, :]
        tile = jnp.broadcast_to(rows[k : k + 1], (LANES, LANES)).T
        lse = jnp.concatenate([tile] * (COLS // LANES), axis=1)
        eye = diagonal(idx, k * LANES, LANES)
        d = jnp.exp(s - lse) + jnp.exp(s - col) - jnp.where(eye, 2.0, 0.0)
        delta[k // 2, (k % 2) * LANES : (k % 2 + 1) * LANES, :] = (fac[0] * d).astype(BF16)
    iaway[0 : ROWS // 2, :] = jnp.dot(delta[1 - c], tx[...], preferred_element_type=F32).astype(BF16)
    put_tail(iaway, ROWS // 2, total)
    whole = delta[...].reshape(ROWS, COLS)
    part[...] = lax.dot_general(
        whole, im[...], (((0,), (0,)), ((), ())), preferred_element_type=F32
    ).reshape(N_Z, N_XL, EACH, WIDTH)
    for z in range(N_Z):
        taway[z * EACH : (z + 1) * EACH, :] = part[z, 1 - xl].astype(BF16)
        there[z * EACH : (z + 1) * EACH, :] = part[z, xl]
    put_tail(taway, COLS // 2, row_loss)


def keep_kernel(idx, delta, tx, ihere):
    ihere[...] = jnp.dot(delta[idx[2]], tx[...], preferred_element_type=F32)


def across_kernel(idx, scal, here, came, away, keep, out):
    half = ROWS // 4
    xh = idx[3]
    go = pl.multiple_of((1 - xh) * half, half)
    stay = pl.multiple_of(xh * half, half)
    total = scal[8:16, :] + value(came[ROWS // 2 : ROWS // 2 + TAIL, 0:LANES])
    out[...] = total
    away[0:half, :] = (here[pl.ds(go, half), :] + came[pl.ds(go, half), :].astype(F32)).astype(BF16)
    put_tail(away, half, total[0:1])
    keep[...] = here[pl.ds(stay, half), :] + came[pl.ds(stay, half), :].astype(F32)


def text_kernel(scal, here, came, out):
    half = COLS // 2
    loss = scal[0:8, :] + value(came[half : half + TAIL, 0:LANES])
    both = (here[...] + came[0:half, :].astype(F32)).astype(BF16)
    tile = pieces(loss[0:1])
    for z in range(N_Z):
        for k in range(SLABS):
            out[z, k * EACH : (k + 1) * EACH, :] = both[z * EACH : (z + 1) * EACH, k * LANES : (k + 1) * LANES]
        out[z, SLABS * EACH :, :] = tile


def ring_kernel(idx, total, keep, got, ahead, behind, near, out):
    y = idx[4]
    half = ROWS // 4
    out[...] = total[...] + value(got[half : half + TAIL, 0:LANES])

    def block(k):
        at = pl.multiple_of(((y + k) & (N_Y - 1)) * EACH, EACH)
        return keep[pl.ds(at, EACH), :] + got[pl.ds(at, EACH), :].astype(F32)

    for n, k in enumerate((1, 4, 6)):
        ahead[n * EACH : (n + 1) * EACH, :] = block(k).astype(BF16)
    for n, k in enumerate((7, 2)):
        behind[n * EACH : (n + 1) * EACH, :] = block(k).astype(BF16)
    for n, k in enumerate((0, 3, 5)):
        near[n * EACH : (n + 1) * EACH, :] = block(k)


def side_kernel(near, low, high, up, down, mid):
    e = EACH
    mid[...] = near[0:e, :] + low[0:e, :].astype(F32) + high[0:e, :].astype(F32)
    up[...] = (near[e : 2 * e, :] + low[e : 2 * e, :].astype(F32) + high[e:, :].astype(F32)).astype(BF16)
    down[...] = (near[2 * e :, :] + low[2 * e :, :].astype(F32)).astype(BF16)


def image_kernel(mid, left, right, out):
    out[...] = (mid[...] + left[...].astype(F32) + right[...].astype(F32)).reshape(EACH, 1, WIDTH)


def final_kernel(got, total, out, loss):
    acc = got[0].astype(F32)
    for z in range(1, N_Z):
        acc = acc + got[z].astype(F32)
    row = acc[SLABS * EACH :]
    acc = jnp.concatenate([acc[k * EACH : (k + 1) * EACH] for k in range(SLABS)], axis=1)
    out[...] = acc.reshape(EACH, 1, WIDTH)
    whole = jnp.sum(jnp.where(lanes((1, LANES)) < 3, row[0:1], 0.0))
    loss[0, 0] = (jnp.max(total[...]) + whole) / (2.0 * PAIRS)


def body(image_emb, text_emb, logit_scale):
    places = [lax.axis_index(a) for a in (ROW, COL, "c", "xh", "y", "xl")]
    idx = jnp.stack(places).astype(jnp.int32)
    (spread,) = call(spread_kernel, [((N_COL, EACH, WIDTH), BF16)], [], idx, image_emb.reshape(EACH, WIDTH))
    images = exchange(spread, ("c", "xh", "y")).reshape(ROWS, WIDTH)
    own = text_emb.reshape(EACH, WIDTH)
    came = shift(own, "xl", 1)
    (texts,) = call(stack_kernel, [((N_XL, EACH, WIDTH), BF16)], [], idx, own, came)
    texts = lax.all_gather(texts, "z").reshape(COLS, WIDTH)
    scores, cpack = call(
        score_kernel,
        [((ROWS, COLS), F32), ((N_ROW, COLS // LANES, LANES), F32)],
        [],
        logit_scale, images, texts,
    )
    col_got = exchange(cpack, ROW)
    (rpack,) = call(row_kernel, [((8, LANES), F32)], [], idx, scores)
    near = lax.all_gather(rpack, ("xh", "c"))
    col_lse, ypack = call(merge_kernel, [((8, COLS), F32), ((N_Y, 8, LANES), F32)], [], col_got, near)
    row_got = exchange(ypack, "y")
    iaway, taway, there, scal, delta = call(
        grad_kernel,
        [
            ((ROWS // 2 + TAIL, WIDTH), BF16),
            ((COLS // 2 + TAIL, WIDTH), BF16),
            ((COLS // 2, WIDTH), F32),
            ((16, LANES), F32),
            ((N_C, ROWS // 2, COLS), BF16),
        ],
        [((N_Z, N_XL, EACH, WIDTH), F32)],
        idx, logit_scale, scores, images, texts, row_got, col_lse,
    )
    tcame = shift(taway, "xl", 1)
    icame = shift(iaway, "c", 1)
    (ihere,) = call(keep_kernel, [((ROWS // 2, WIDTH), F32)], [], idx, delta, texts)
    xaway, keep, total = call(
        across_kernel,
        [((ROWS // 4 + TAIL, WIDTH), BF16), ((ROWS // 4, WIDTH), F32), ((8, LANES), F32)],
        [],
        idx, scal, ihere, icame,
    )
    xcame = shift(xaway, "xh", 1)
    (tpack,) = call(text_kernel, [((N_Z, SLABS * EACH + TAIL, LANES), BF16)], [], scal, there, tcame)
    text_got = exchange(tpack, "z")
    ahead, behind, near3, total = call(
        ring_kernel,
        [((3 * EACH, WIDTH), BF16), ((2 * EACH, WIDTH), BF16), ((3 * EACH, WIDTH), F32), ((8, LANES), F32)],
        [],
        idx, total, keep, xcame,
    )
    low = shift(ahead, "y", 1)
    high = shift(behind, "y", 7)
    up, down, mid = call(
        side_kernel,
        [((EACH, WIDTH), BF16), ((EACH, WIDTH), BF16), ((EACH, WIDTH), F32)],
        [],
        near3, low, high,
    )
    left = shift(up, "y", 3)
    right = shift(down, "y", 5)
    text_grad, loss = call(final_kernel, [((EACH, 1, WIDTH), F32), ((1, 1), F32)], [], text_got, total)
    (image_grad,) = call(image_kernel, [((EACH, 1, WIDTH), F32)], [], mid, left, right)
    return loss[0, 0], image_grad, text_grad


def solution(mesh):
    fine = Mesh(mesh.devices.reshape(N_XL, N_Z, N_Y, N_XH, N_C), ROW + COL)
    placed = (P(ROW, COL, None), P(COL, ROW, None), P())
    return jax.shard_map(
        body,
        mesh=fine,
        in_specs=placed,
        out_specs=(P(), P(ROW, COL, None), P(COL, ROW, None)),
        check_vma=False,
    )
```
